32 devices in a mesh: groups: 2 (over y), patch: 4 (over z), view: 2 (over x), head: 2 (over core).
Axes of the slice: x: 2, y: 2, z: 4, core: 2. Of those that a mesh axis runs over, the one named last changes fastest.
Arguments:
- tokens: bfloat16 [8192, 768], P(('groups', 'patch', 'view', 'head')), parts along dimension 0, may hold values from -6 to 6
- w_kv: bfloat16 [768, 1536], replicated, may hold values from -0.21875 to 0.21875
- w_rate: bfloat16 [3, 768], replicated, may hold values from -0.21875 to 0.21875
- fast_weights: bfloat16 [512, 3, 3, 256], replicated, as said below
- queries: bfloat16 [8192, 768], P(('groups', 'patch', 'view', 'head')), parts along dimension 0, may hold values from -6 to 6
- w_query: bfloat16 [768, 768], replicated, may hold values from -0.21875 to 0.21875
- out_gain: bfloat16 [768], replicated, may hold values from 0.25 to 1.75
- w_out: bfloat16 [768, 768], replicated, may hold values from -0.21875 to 0.21875
Outputs:
- decoded: bfloat16 [8192, 768], P(('groups', 'patch', 'view', 'head')), parts along dimension 0
The draws below stay inside these ranges and needn't reach their ends.
There are 2 independent parts, one for each index of `groups`. The reference program is written for one: setup_inputs(seed, part) draws one part's arguments, and reference() takes and returns one part's arrays. A program takes and returns all parts, laid end to end along the dimension named above; an argument that names none is the same for every part. Nothing has to cross between parts.
Inputs may be any that keep to these rules, and one draw needn't show every extreme that they name: `fast_weights`: Real-valued entries.
All inputs are finite; a program needn't handle non-finite values.
Results may differ from the reference program's by a relative error of at most 0.035.
Values may be sent and summed in bfloat16 or wider, within the bound.
No kernel may reach another device: no remote copies, remote signals or barrier semaphores. Data moves between devices by JAX's collectives and lax.ppermute only.
A program may use at most 64 MiB of HBM per device.

```python
import math
import jax
import jax.numpy as jnp
from jax import lax

HEADS = 3
HD = 256
FF = 512
D = 768
TOK_DEV = 256
QRY_DEV = 256
STEPS = 3
TOKENS = 4096
QUERIES = 4096
N_HEAD = 2


def draw_fast_weights(key, part):
    shape = (FF, 3, HEADS, HD)
    base = jnp.clip(jax.random.normal(key, shape, jnp.float32), -4.0, 4.0)
    rise = math.log(3.0)
    position = jnp.arange(FF, dtype=jnp.float32) / (FF - 1)
    factor = jnp.exp(rise * position)[:, None, None, None]
    return (base * factor * HD ** (-0.5)).astype(jnp.bfloat16)


def shard_levels(own_key, extent, shards, least, high):
    loudness = 1.0
    for dim, blocks in shards:
        heights = jax.random.uniform(jax.random.fold_in(jax.random.fold_in(own_key, 6), dim), (blocks,), jnp.float32, least / len(shards), high / len(shards))
        loudness = loudness * jnp.repeat(jnp.exp(heights), extent[dim] // blocks).reshape((-1,) + (1,) * (len(extent) - 1 - dim))
    return loudness


def normal_values(stream_key, dims, scale, most, shards=(), kind=jnp.bfloat16):
    entries = scale * jax.random.normal(stream_key, dims, jnp.float32)
    if shards:
        entries = entries * shard_levels(stream_key, dims, shards, -0.22, 0.18)
    return jnp.clip(entries, -most, most).astype(kind)


def setup_inputs(seed: int = 0, part: int = 0) -> dict:
    key_of = jax.random.split(jax.random.key(seed), 9)
    part_splits = jax.random.split(jax.random.fold_in(key_of[8], part), 9)
    return {
        "tokens": normal_values(part_splits[0], (TOKENS, D), 1.0, 6.0, ((0, 16),)),
        "w_kv": normal_values(key_of[1], (D, 2 * D), D ** -0.5, 0.21875),
        "w_rate": normal_values(key_of[2], (HEADS, D), D ** -0.5, 0.21875),
        "fast_weights": draw_fast_weights(jax.random.fold_in(key_of[8], 71), part),
        "queries": normal_values(part_splits[4], (QUERIES, D), 1.0, 6.0, ((0, 16),)),
        "w_query": normal_values(key_of[5], (D, D), D ** -0.5, 0.21875),
        "out_gain": jnp.clip(1.0 + 0.15 * jax.random.normal(key_of[6], (D,), jnp.float32), 0.25, 1.75).astype(jnp.bfloat16),
        "w_out": normal_values(key_of[7], (D, D), D ** -0.5, 0.21875),
    }


coef_a = 3.4445
coef_b = -4.775
coef_c = 2.0315
eta_rate = 3.0
eps_small = 1e-06

def unit_heads(raw):
    shaped = raw.reshape(raw.shape[0], HEADS, HD)
    return shaped / jnp.sqrt(lax.optimization_barrier(jnp.sum(shaped * shaped, -1, keepdims=True)) + eps_small)

def reference(tokens, w_kv, w_rate, fast_weights, queries, w_query, out_gain, w_out):
    fp = jnp.float32
    width = HEADS * HD
    fast = fast_weights.astype(fp)
    block = TOK_DEV * N_HEAD

    def grad_block(total, index):
        xrows = lax.dynamic_slice_in_dim(tokens, (index * block).astype(jnp.int32), block, 0)
        both = jnp.dot(xrows, w_kv, preferred_element_type=fp)
        keys = unit_heads(both[:, :width]).astype(jnp.bfloat16).astype(fp)
        rate = jax.nn.softplus(jnp.dot(xrows, w_rate.T, preferred_element_type=fp))
        scaled = (rate[:, :, None] * both[:, width:].reshape(-1, HEADS, HD)).astype(jnp.bfloat16).astype(fp)
        gate_pre = jnp.einsum('thd,nhd->hnt', keys, fast[:, 0])
        up_pre = jnp.einsum('thd,nhd->hnt', keys, fast[:, 1])
        sig = jax.nn.sigmoid(gate_pre)
        act = gate_pre * sig
        hidden = (act * up_pre).astype(jnp.bfloat16).astype(fp)
        back = jnp.einsum('thd,nhd->hnt', scaled, fast[:, 2])
        d_gate = (back * up_pre * sig * (1.0 + gate_pre * (1.0 - sig))).astype(jnp.bfloat16).astype(fp)
        d_up = (back * act).astype(jnp.bfloat16).astype(fp)
        g_gate = jnp.einsum('hnt,thd->nhd', d_gate, keys)
        g_up = jnp.einsum('hnt,thd->nhd', d_up, keys)
        g_down = jnp.einsum('hnt,thd->nhd', hidden, scaled)
        return (total + jnp.stack([g_gate, g_up, g_down], 1), None)
    grads, _ = lax.scan(grad_block, jnp.zeros((FF, 3, HEADS, HD), fp), jnp.arange(TOKENS // block, dtype=jnp.int32))
    total = lax.optimization_barrier(jnp.sum(grads * grads, axis=(0, 3)))
    ortho = (grads / (jnp.sqrt(total) + eps_small)[None, :, :, None]).astype(jnp.bfloat16)
    for step in range(STEPS):
        xf = ortho.astype(fp)
        gram = jnp.einsum('nkhi,nkhj->khij', xf, xf).astype(jnp.bfloat16).astype(fp)
        square = jnp.einsum('khij,khjl->khil', gram, gram)
        poly = (coef_b * gram + coef_c * square).astype(jnp.bfloat16).astype(fp)
        ortho = (coef_a * xf + jnp.einsum('nkhi,khij->nkhj', xf, poly)).astype(jnp.bfloat16)
    moved = fast + eta_rate * ortho.astype(fp)
    old_norm = jnp.sqrt(lax.optimization_barrier(jnp.sum(fast * fast, -1, keepdims=True)))
    new_norm = jnp.sqrt(lax.optimization_barrier(jnp.sum(moved * moved, -1, keepdims=True))) + eps_small
    fresh = (moved * old_norm / new_norm).astype(jnp.bfloat16).astype(fp)
    qblock = QRY_DEV * N_HEAD

    def decode_block(index):
        qrows = lax.dynamic_slice_in_dim(queries, (index * qblock).astype(jnp.int32), qblock, 0)
        qry = unit_heads(jnp.dot(qrows, w_query, preferred_element_type=fp)).astype(jnp.bfloat16).astype(fp)
        gate_pre = jnp.einsum('thd,nhd->hnt', qry, fresh[:, 0])
        up_pre = jnp.einsum('thd,nhd->hnt', qry, fresh[:, 1])
        q_hidden = (jax.nn.silu(gate_pre) * up_pre).astype(jnp.bfloat16).astype(fp)
        read = jnp.einsum('hnt,nhd->thd', q_hidden, fresh[:, 2])
        normed = read / jnp.sqrt(lax.optimization_barrier(jnp.mean(read * read, -1, keepdims=True)) + eps_small)
        normed = normed * out_gain.astype(fp).reshape(HEADS, HD)
        normed = normed.reshape(qblock, width).astype(jnp.bfloat16)
        return jnp.dot(normed, w_out, preferred_element_type=fp).astype(jnp.bfloat16)
    blocks = lax.map(decode_block, jnp.arange(QUERIES // qblock, dtype=jnp.int32))
    return blocks.reshape(QUERIES, width)
```

```python
import functools
import jax
import jax.numpy as jnp
from jax import lax
from jax.experimental import pallas as pl
from jax.experimental.pallas import tpu as pltpu
from jax.sharding import PartitionSpec as P

HEADS = 3
HD = 256
FF = 512
STEPS = 3

coef_a = 3.4445
coef_b = -4.775
coef_c = 2.0315
eta_rate = 3.0
eps_small = 1e-06

FP = jnp.float32
BF = jnp.bfloat16
NT = (((1,), (1,)), ((), ()))
TN = (((0,), (0,)), ((), ()))
ROWS = 3 * FF


def mm(a, b, dims=(((1,), (0,)), ((), ()))):
    return lax.dot_general(a, b, dims, preferred_element_type=FP)


def unit(raw):
    return raw * lax.rsqrt(jnp.sum(raw * raw, -1, keepdims=True) + eps_small)


def add_gradient(tok, head, w_k, w_v, w_rate, fast, acc):
    rows = tok[...]
    keys = unit(mm(rows, w_k[...])).astype(BF)
    rates = mm(rows, w_rate[...], NT)
    pick = lax.broadcasted_iota(jnp.int32, rates.shape, 1) == head
    rate = jnp.sum(jnp.where(pick, rates, 0.0), -1, keepdims=True)
    rate = jnp.maximum(rate, 0.0) + jnp.log1p(jnp.exp(-jnp.abs(rate)))
    scaled = (rate * mm(rows, w_v[...])).astype(BF)
    gate_pre = mm(fast[0], keys, NT)
    up_pre = mm(fast[1], keys, NT)
    back = mm(fast[2], scaled, NT)
    sig = jax.nn.sigmoid(gate_pre)
    act = gate_pre * sig
    hidden = (act * up_pre).astype(BF)
    d_gate = (back * up_pre * sig * (1.0 + gate_pre * (1.0 - sig))).astype(BF)
    d_up = (back * act).astype(BF)
    acc[0:FF] += mm(d_gate, keys)
    acc[FF : 2 * FF] += mm(d_up, keys)
    acc[2 * FF : ROWS] += mm(hidden, scaled)


def first_kernel(n_tok, where, *refs):
    toks, (w_k, w_v, w_rate, fast, acc) = refs[:n_tok], refs[n_tok:]
    acc[...] = jnp.zeros_like(acc)
    for tok in toks:
        add_gradient(tok, where[0], w_k, w_v, w_rate, fast, acc)


def second_kernel(n_tok, n_patch, where, *refs):
    toks, (w_k, w_v, w_rate, fast, begun) = refs[:n_tok], refs[n_tok : n_tok + 5]
    outs, acc = refs[n_tok + 5 : -1], refs[-1]
    acc[...] = begun[...]
    for tok in toks:
        add_gradient(tok, where[0], w_k, w_v, w_rate, fast, acc)
    size = ROWS // n_patch
    for shift, out in enumerate(outs):
        chunk = lax.rem(where[1] + shift, n_patch)
        out[...] = acc[pl.ds(pl.multiple_of(chunk * size, size), size)].astype(out.dtype)


def decode_kernel(n_patch, where, *refs):
    parts, (fast, gain, qry, out, grads, fresh) = refs[:n_patch], refs[n_patch:]
    size = ROWS // n_patch
    for shift, part in enumerate(parts):
        chunk = lax.rem(where[1] + n_patch - shift, n_patch)
        grads[pl.ds(pl.multiple_of(chunk * size, size), size)] = part[...]
    ortho = []
    for kind in range(3):
        grad = grads[kind * FF : (kind + 1) * FF].astype(FP)
        total = jnp.sum(jnp.sum(grad * grad, -1, keepdims=True), 0, keepdims=True)
        ortho.append((grad / (jnp.sqrt(total) + eps_small)).astype(BF))
    for step in range(STEPS):
        gram = [mm(x, x, TN).astype(BF) for x in ortho]
        square = [mm(g, g) for g in gram]
        poly = [(coef_b * g.astype(FP) + coef_c * s).astype(BF) for g, s in zip(gram, square)]
        mixed = [mm(x, p) for x, p in zip(ortho, poly)]
        ortho = [(coef_a * x.astype(FP) + m).astype(BF) for x, m in zip(ortho, mixed)]
    for kind in range(3):
        old = fast[kind].astype(FP)
        moved = old + eta_rate * ortho[kind].astype(FP)
        old_norm = jnp.sqrt(jnp.sum(old * old, -1, keepdims=True))
        new_norm = jnp.sqrt(jnp.sum(moved * moved, -1, keepdims=True)) + eps_small
        fresh[kind] = (moved * (old_norm / new_norm)).astype(BF)
    block = HD
    for start in range(0, qry.shape[0], block):
        rows = qry[start : start + block]
        gate_pre = mm(rows, fresh[0], NT)
        up_pre = mm(rows, fresh[1], NT)
        hidden = (gate_pre * jax.nn.sigmoid(gate_pre) * up_pre).astype(BF)
        read = mm(hidden, fresh[2])
        normed = read * lax.rsqrt(jnp.mean(read * read, -1, keepdims=True) + eps_small)
        out[start : start + block] = (normed * gain[...].astype(FP)).astype(BF)


def whole(*shape):
    return pl.BlockSpec(shape, lambda i, where: (0,) * len(shape))


def call(kernel, where, args, specs, outs, scratch=()):
    return pl.pallas_call(
        kernel,
        out_shape=outs,
        grid_spec=pltpu.PrefetchScalarGridSpec(
            num_scalar_prefetch=1,
            grid=(1,),
            in_specs=specs,
            out_specs=jax.tree.map(lambda o: whole(*o.shape), outs),
            scratch_shapes=scratch,
        ),
        compiler_params=pltpu.CompilerParams(vmem_limit_bytes=40 << 20),
    )(where, *args)


def unit_heads(raw):
    return unit(raw.reshape(raw.shape[0], HEADS, HD))


def local(tokens, w_kv, w_rate, fast_weights, queries, w_query, out_gain, w_out):
    n_patch, n_view, n_head = (lax.axis_size(a) for a in ("patch", "view", "head"))
    patch, view, core = (lax.axis_index(a) for a in ("patch", "view", "head"))
    n_tok, width = tokens.shape
    n_qry = queries.shape[0]
    side = view % 2
    head = jnp.where(core == 1, 1, 2 * side).astype(jnp.int32)
    where = jnp.stack([head, patch.astype(jnp.int32)])
    swap = [(0, 1), (1, 0)]
    flip = [(i, i ^ 1) for i in range(n_view)]
    first = [(v * n_head, (v ^ 1) * n_head) for v in range(n_view)]

    def rotate(n, shift):
        return [(i, (i + shift) % n) for i in range(n)]

    far = [lax.ppermute(tokens, "view", rotate(n_view, s)) for s in range(1, n_view)]
    near = [tokens, lax.ppermute(tokens, "head", swap)]
    far = far + [lax.ppermute(f, "head", swap) for f in far]
    mine = lax.dynamic_index_in_dim(fast_weights, head, 2, keepdims=False).transpose(1, 0, 2)

    weights = [w_kv, w_kv, w_rate, mine]
    weight_specs = [
        pl.BlockSpec((width, HD), lambda i, where: (0, where[0])),
        pl.BlockSpec((width, HD), lambda i, where: (0, HEADS + where[0])),
        whole(HEADS, width),
        whole(3, FF, HD),
    ]
    begun = call(
        functools.partial(first_kernel, len(near)),
        where,
        near + weights,
        [whole(n_tok, width)] * len(near) + weight_specs,
        jax.ShapeDtypeStruct((ROWS, HD), FP),
    )
    size = ROWS // n_patch
    chunks = call(
        functools.partial(second_kernel, len(far), n_patch),
        where,
        far + weights + [begun],
        [whole(n_tok, width)] * len(far) + weight_specs + [whole(ROWS, HD)],
        [jax.ShapeDtypeStruct((size, HD), BF if s else FP) for s in range(n_patch)],
        [pltpu.VMEM((ROWS, HD), FP)],
    )
    order = sorted(range(1, n_patch), key=lambda s: -min(s, n_patch - s))
    got = {s: lax.ppermute(chunks[s], "patch", rotate(n_patch, s)) for s in order}
    own = chunks[0]
    for s in order:
        own = own + got[s].astype(FP)
    own = own.astype(BF)
    parts = {s: lax.ppermute(own, "patch", rotate(n_patch, s)) for s in order}

    qry = unit_heads(jnp.dot(queries, w_query, preferred_element_type=FP)).astype(BF)
    pair = jnp.where(side == 0, qry[:, 0], qry[:, 2])
    other = jnp.where(side == 0, qry[:, 2], qry[:, 0])
    out_first = jnp.where(core == 0, qry[:, 1], pair)
    own_qry = jnp.where(core == 0, pair, qry[:, 1])
    swapped = lax.ppermute(jnp.concatenate([out_first, other]), "head", swap)
    across = lax.ppermute(jnp.concatenate([other, swapped[n_qry:]]), ("view", "head"), first)
    all_qry = jnp.concatenate([own_qry, swapped[:n_qry], across])

    normed = call(
        functools.partial(decode_kernel, n_patch),
        where,
        [own] + [parts[s] for s in range(1, n_patch)] + [mine, out_gain.reshape(1, width), all_qry],
        [whole(size, HD)] * n_patch
        + [
            whole(3, FF, HD),
            pl.BlockSpec((1, HD), lambda i, where: (0, where[0])),
            whole(4 * n_qry, HD),
        ],
        jax.ShapeDtypeStruct((4 * n_qry, HD), BF),
        [pltpu.VMEM((ROWS, HD), BF), pltpu.VMEM((3, FF, HD), BF)],
    )
    back = lax.ppermute(normed[2 * n_qry :], ("view", "head"), first)
    sib = lax.ppermute(normed[n_qry : 2 * n_qry], "head", swap)
    relayed = lax.ppermute(back[n_qry:], "head", swap)
    own_out = normed[:n_qry]
    one = jnp.where(core == 0, sib, own_out)
    same = jnp.where(core == 0, own_out, sib)
    cross = jnp.where(core == 0, back[:n_qry], relayed)
    zero = jnp.where(side == 0, same, cross)
    two = jnp.where(side == 0, cross, same)
    joined = jnp.concatenate([zero, one, two], 1)
    return jnp.dot(joined, w_out, preferred_element_type=FP).astype(BF)


def solution(mesh):
    split = P(("groups", "patch", "view", "head"), None)
    in_specs = (split, P(), P(), P(), split, P(), P(), P())
    return jax.shard_map(local, mesh=mesh, in_specs=in_specs, out_specs=split, check_vma=False)
```

```python
import functools
import jax
import jax.numpy as jnp
from jax import lax
from jax.experimental import pallas as pl
from jax.experimental.pallas import tpu as pltpu
from jax.sharding import PartitionSpec as P

HEADS = 3
HD = 256
FF = 512
STEPS = 3

coef_a = 3.4445
coef_b = -4.775
coef_c = 2.0315
eta_rate = 3.0
eps_small = 1e-06

FP = jnp.float32
BF = jnp.bfloat16
NT = (((1,), (1,)), ((), ()))
TN = (((0,), (0,)), ((), ()))
ROWS = 3 * FF


def mm(a, b, dims=(((1,), (0,)), ((), ()))):
    return lax.dot_general(a, b, dims, preferred_element_type=FP)


def unit(raw):
    return raw * lax.rsqrt(jnp.sum(raw * raw, -1, keepdims=True) + eps_small)


def add_gradient(tok, head, w_k, w_v, w_rate, fast, acc):
    rows = tok[...]
    keys = unit(mm(rows, w_k[...])).astype(BF)
    rates = mm(rows, w_rate[...], NT)
    pick = lax.broadcasted_iota(jnp.int32, rates.shape, 1) == head
    rate = jnp.sum(jnp.where(pick, rates, 0.0), -1, keepdims=True)
    rate = jnp.maximum(rate, 0.0) + jnp.log1p(jnp.exp(-jnp.abs(rate)))
    scaled = (rate * mm(rows, w_v[...])).astype(BF)
    gate_pre = mm(fast[0], keys, NT)
    up_pre = mm(fast[1], keys, NT)
    back = mm(fast[2], scaled, NT)
    sig = jax.nn.sigmoid(gate_pre)
    act = gate_pre * sig
    hidden = (act * up_pre).astype(BF)
    d_gate = (back * up_pre * sig * (1.0 + gate_pre * (1.0 - sig))).astype(BF)
    d_up = (back * act).astype(BF)
    acc[0:FF] += mm(d_gate, keys)
    acc[FF : 2 * FF] += mm(d_up, keys)
    acc[2 * FF : ROWS] += mm(hidden, scaled)


def first_kernel(n_tok, where, *refs):
    toks, (w_k, w_v, w_rate, fast, acc) = refs[:n_tok], refs[n_tok:]
    acc[...] = jnp.zeros_like(acc)
    for tok in toks:
        add_gradient(tok, where[0], w_k, w_v, w_rate, fast, acc)


def second_kernel(n_tok, n_patch, where, *refs):
    toks, (w_k, w_v, w_rate, fast, begun) = refs[:n_tok], refs[n_tok : n_tok + 5]
    outs, acc = refs[n_tok + 5 : -1], refs[-1]
    acc[...] = begun[...]
    for tok in toks:
        add_gradient(tok, where[0], w_k, w_v, w_rate, fast, acc)
    size = ROWS // n_patch
    for shift, out in enumerate(outs):
        chunk = lax.rem(where[1] + shift, n_patch)
        out[...] = acc[pl.ds(pl.multiple_of(chunk * size, size), size)].astype(out.dtype)


def decode_kernel(n_patch, where, *refs):
    parts, (fast, gain, *queries, out, grads, fresh) = refs[:n_patch], refs[n_patch:]
    size = ROWS // n_patch
    for shift, part in enumerate(parts):
        chunk = lax.rem(where[1] + n_patch - shift, n_patch)
        grads[pl.ds(pl.multiple_of(chunk * size, size), size)] = part[...]
    ortho = []
    for kind in range(3):
        grad = grads[kind * FF : (kind + 1) * FF].astype(FP)
        total = jnp.sum(jnp.sum(grad * grad, -1, keepdims=True), 0, keepdims=True)
        ortho.append((grad / (jnp.sqrt(total) + eps_small)).astype(BF))
    for step in range(STEPS):
        gram = [mm(x, x, TN).astype(BF) for x in ortho]
        square = [mm(g, g) for g in gram]
        poly = [(coef_b * g.astype(FP) + coef_c * s).astype(BF) for g, s in zip(gram, square)]
        mixed = [mm(x, p) for x, p in zip(ortho, poly)]
        ortho = [(coef_a * x.astype(FP) + m).astype(BF) for x, m in zip(ortho, mixed)]
    for kind in range(3):
        old = fast[kind].astype(FP)
        moved = old + eta_rate * ortho[kind].astype(FP)
        old_norm = jnp.sqrt(jnp.sum(old * old, -1, keepdims=True))
        new_norm = jnp.sqrt(jnp.sum(moved * moved, -1, keepdims=True)) + eps_small
        fresh[kind] = (moved * (old_norm / new_norm)).astype(BF)
    start = 0
    for qry in queries:
        for row in range(0, qry.shape[0], HD):
            rows = qry[row : row + HD]
            gate_pre = mm(rows, fresh[0], NT)
            up_pre = mm(rows, fresh[1], NT)
            hidden = (gate_pre * jax.nn.sigmoid(gate_pre) * up_pre).astype(BF)
            read = mm(hidden, fresh[2])
            normed = read * lax.rsqrt(jnp.mean(read * read, -1, keepdims=True) + eps_small)
            out[start : start + HD] = (normed * gain[...].astype(FP)).astype(BF)
            start += HD


def query_kernel(where, queries, w_query, own, message, other, heads):
    rows = mm(queries[...], w_query[...])
    for head in range(HEADS):
        heads[head] = unit(rows[:, head * HD : (head + 1) * HD]).astype(BF)
    n_qry = own.shape[0]
    own[...] = heads[where[0]]
    message[:n_qry] = heads[where[2]]
    message[n_qry:] = heads[where[3]]
    other[...] = heads[where[3]]


def whole(*shape):
    return pl.BlockSpec(shape, lambda i, where: (0,) * len(shape))


def call(kernel, where, args, specs, outs, scratch=()):
    return pl.pallas_call(
        kernel,
        out_shape=outs,
        grid_spec=pltpu.PrefetchScalarGridSpec(
            num_scalar_prefetch=1,
            grid=(1,),
            in_specs=specs,
            out_specs=jax.tree.map(lambda o: whole(*o.shape), outs),
            scratch_shapes=scratch,
        ),
        compiler_params=pltpu.CompilerParams(vmem_limit_bytes=40 << 20),
    )(where, *args)


def local(tokens, w_kv, w_rate, fast_weights, queries, w_query, out_gain, w_out):
    n_patch, n_view, n_head = (lax.axis_size(a) for a in ("patch", "view", "head"))
    patch, view, core = (lax.axis_index(a) for a in ("patch", "view", "head"))
    n_tok, width = tokens.shape
    n_qry = queries.shape[0]
    side = view % 2
    head = jnp.where(core == 1, 1, 2 * side)
    sibling = jnp.where(core == 1, 2 * side, 1)
    where = jnp.stack([head, patch, sibling, 2 - 2 * side]).astype(jnp.int32)
    swap = [(0, 1), (1, 0)]
    flip = [(i, i ^ 1) for i in range(n_view)]
    first = [(v * n_head, (v ^ 1) * n_head) for v in range(n_view)]

    def rotate(n, shift):
        return [(i, (i + shift) % n) for i in range(n)]

    far = [lax.ppermute(tokens, "view", rotate(n_view, s)) for s in range(1, n_view)]
    near = [tokens, lax.ppermute(tokens, "head", swap)]
    mine = lax.dynamic_index_in_dim(fast_weights, head, 2, keepdims=False).transpose(1, 0, 2)

    w_k = lax.dynamic_slice_in_dim(w_kv, head * HD, HD, 1)
    w_v = lax.dynamic_slice_in_dim(w_kv, width + head * HD, HD, 1)

    weights = [w_k, w_v, w_rate, mine]
    weight_specs = [
        whole(width, HD),
        whole(width, HD),
        whole(HEADS, width),
        whole(3, FF, HD),
    ]
    begun = call(
        functools.partial(first_kernel, len(near)),
        where,
        near + weights,
        [whole(n_tok, width)] * len(near) + weight_specs,
        jax.ShapeDtypeStruct((ROWS, HD), FP),
    )
    begun, *far = lax.optimization_barrier((begun, *far))
    far = far + [lax.ppermute(f, "head", swap) for f in far]
    size = ROWS // n_patch
    chunks = call(
        functools.partial(second_kernel, len(far), n_patch),
        where,
        far + weights + [begun],
        [whole(n_tok, width)] * len(far) + weight_specs + [whole(ROWS, HD)],
        [jax.ShapeDtypeStruct((size, HD), BF if s else FP) for s in range(n_patch)],
        [pltpu.VMEM((ROWS, HD), FP)],
    )
    order = sorted(range(1, n_patch), key=lambda s: -min(s, n_patch - s))
    got = {s: lax.ppermute(chunks[s], "patch", rotate(n_patch, s)) for s in order}
    own = chunks[0]
    for s in order:
        own = own + got[s].astype(FP)
    own = own.astype(BF)
    parts = {s: lax.ppermute(own, "patch", rotate(n_patch, s)) for s in order}

    late, _ = lax.optimization_barrier((queries, chunks[0]))
    own_qry, message, other = call(
        query_kernel,
        where,
        [late, w_query],
        [whole(n_qry, width), whole(width, width)],
        [jax.ShapeDtypeStruct((n, HD), BF) for n in (n_qry, 2 * n_qry, n_qry)],
        [pltpu.VMEM((HEADS, n_qry, HD), BF)],
    )
    swapped = lax.ppermute(message, "head", swap)
    across = lax.ppermute(jnp.concatenate([other, swapped[n_qry:]]), ("view", "head"), first)

    normed = call(
        functools.partial(decode_kernel, n_patch),
        where,
        [own] + [parts[s] for s in range(1, n_patch)]
        + [mine, out_gain.reshape(1, width), own_qry, swapped, across],
        [whole(size, HD)] * n_patch
        + [
            whole(3, FF, HD),
            pl.BlockSpec((1, HD), lambda i, where: (0, where[0])),
            whole(n_qry, HD),
            whole(n_qry, HD),
            whole(2 * n_qry, HD),
        ],
        jax.ShapeDtypeStruct((4 * n_qry, HD), BF),
        [pltpu.VMEM((ROWS, HD), BF), pltpu.VMEM((3, FF, HD), BF)],
    )
    back = lax.ppermute(normed[2 * n_qry :], ("view", "head"), first)
    sib = lax.ppermute(normed[n_qry : 2 * n_qry], "head", swap)
    relayed = lax.ppermute(back[n_qry:], "head", swap)
    own_out = normed[:n_qry]
    one = jnp.where(core == 0, sib, own_out)
    same = jnp.where(core == 0, own_out, sib)
    cross = jnp.where(core == 0, back[:n_qry], relayed)
    zero = jnp.where(side == 0, same, cross)
    two = jnp.where(side == 0, cross, same)
    joined = jnp.concatenate([zero, one, two], 1)
    return jnp.dot(joined, w_out, preferred_element_type=FP).astype(BF)


def solution(mesh):
    split = P(("groups", "patch", "view", "head"), None)
    in_specs = (split, P(), P(), P(), split, P(), P(), P())
    return jax.shard_map(local, mesh=mesh, in_specs=in_specs, out_specs=split, check_vma=False)
```

```python
import functools
import jax
import jax.numpy as jnp
from jax import lax
from jax.experimental import pallas as pl
from jax.experimental.pallas import tpu as pltpu
from jax.sharding import PartitionSpec as P

HEADS = 3
HD = 256
FF = 512
STEPS = 3

coef_a = 3.4445
coef_b = -4.775
coef_c = 2.0315
eta_rate = 3.0
eps_small = 1e-06

FP = jnp.float32
BF = jnp.bfloat16
NT = (((1,), (1,)), ((), ()))
TN = (((0,), (0,)), ((), ()))
ROWS = 3 * FF


def mm(a, b, dims=(((1,), (0,)), ((), ()))):
    return lax.dot_general(a, b, dims, preferred_element_type=FP)


def unit(raw):
    return raw * lax.rsqrt(jnp.sum(raw * raw, -1, keepdims=True) + eps_small)


def peer(index, shift):
    return index ^ shift


def add_gradient(tok, head, w_k, w_v, w_rate, fast, acc):
    rows = tok[...]
    keys = unit(mm(rows, w_k[...])).astype(BF)
    rates = mm(rows, w_rate[...], NT)
    pick = lax.broadcasted_iota(jnp.int32, rates.shape, 1) == head
    rate = jnp.sum(jnp.where(pick, rates, 0.0), -1, keepdims=True)
    rate = jnp.maximum(rate, 0.0) + jnp.log1p(jnp.exp(-jnp.abs(rate)))
    scaled = (rate * mm(rows, w_v[...])).astype(BF)
    gate_pre = mm(fast[0], keys, NT)
    up_pre = mm(fast[1], keys, NT)
    back = mm(fast[2], scaled, NT)
    sig = jax.nn.sigmoid(gate_pre)
    act = gate_pre * sig
    hidden = (act * up_pre).astype(BF)
    d_gate = (back * up_pre * sig * (1.0 + gate_pre * (1.0 - sig))).astype(BF)
    d_up = (back * act).astype(BF)
    acc[0:FF] += mm(d_gate, keys)
    acc[FF : 2 * FF] += mm(d_up, keys)
    acc[2 * FF : ROWS] += mm(hidden, scaled)


def first_kernel(n_tok, where, *refs):
    toks, (w_k, w_v, w_rate, fast, acc) = refs[:n_tok], refs[n_tok:]
    acc[...] = jnp.zeros_like(acc)
    for tok in toks:
        add_gradient(tok, where[0], w_k, w_v, w_rate, fast, acc)


def second_kernel(n_tok, n_patch, where, *refs):
    toks, (w_k, w_v, w_rate, fast, begun) = refs[:n_tok], refs[n_tok : n_tok + 5]
    outs, acc = refs[n_tok + 5 : -1], refs[-1]
    acc[...] = begun[...]
    for tok in toks:
        add_gradient(tok, where[0], w_k, w_v, w_rate, fast, acc)
    size = ROWS // n_patch
    for shift, out in enumerate(outs):
        chunk = peer(where[1], shift)
        out[...] = acc[pl.ds(pl.multiple_of(chunk * size, size), size)].astype(out.dtype)


def decode(rows, fresh, gain):
    gate_pre = mm(rows, fresh[0], NT)
    up_pre = mm(rows, fresh[1], NT)
    hidden = (gate_pre * jax.nn.sigmoid(gate_pre) * up_pre).astype(BF)
    read = mm(hidden, fresh[2])
    return (read * lax.rsqrt(jnp.mean(read * read, -1, keepdims=True) + eps_small) * gain).astype(BF)


def own_gain(gains, head):
    low, middle, high = (gains[:, i * HD : (i + 1) * HD] for i in range(HEADS))
    return jnp.where(head == 0, low, jnp.where(head == 1, middle, high)).astype(FP)


def near_kernel(where, own, other, fresh, gains, w_out, for_other, begun):
    gain = own_gain(gains, where[0])
    for_other[...] = decode(other[...], fresh, gain)
    product = w_out[pl.ds(pl.multiple_of(where[0] * HD, HD), HD)]
    begun[...] = mm(decode(own[...], fresh, gain), product)


def far_kernel(n_patch, order, where, *refs):
    parts, (fast, gains, qry, out, fresh, grads) = refs[:n_patch], refs[n_patch:]
    size = ROWS // n_patch
    for shift, part in zip((0, *order), parts):
        chunk = peer(where[1], shift)
        grads[pl.ds(pl.multiple_of(chunk * size, size), size)] = part[...]
    ortho = []
    for kind in range(3):
        grad = grads[kind * FF : (kind + 1) * FF].astype(FP)
        total = jnp.sum(jnp.sum(grad * grad, -1, keepdims=True), 0, keepdims=True)
        ortho.append((grad / (jnp.sqrt(total) + eps_small)).astype(BF))
    for step in range(STEPS):
        gram = [mm(x, x, TN).astype(BF) for x in ortho]
        square = [mm(g, g) for g in gram]
        poly = [(coef_b * g.astype(FP) + coef_c * s).astype(BF) for g, s in zip(gram, square)]
        mixed = [mm(x, p) for x, p in zip(ortho, poly)]
        ortho = [(coef_a * x.astype(FP) + m).astype(BF) for x, m in zip(ortho, mixed)]
    for kind in range(3):
        old = fast[kind].astype(FP)
        moved = old + eta_rate * ortho[kind].astype(FP)
        old_norm = jnp.sqrt(jnp.sum(old * old, -1, keepdims=True))
        new_norm = jnp.sqrt(jnp.sum(moved * moved, -1, keepdims=True)) + eps_small
        fresh[kind] = (moved * (old_norm / new_norm)).astype(BF)
    gain = own_gain(gains, where[0])
    for row in range(0, qry.shape[0], HD):
        out[row : row + HD] = decode(qry[row : row + HD], fresh, gain)


def query_kernel(where, queries, w_query, own, message, other, heads):
    rows = mm(queries[...], w_query[...])
    for head in range(HEADS):
        heads[head] = unit(rows[:, head * HD : (head + 1) * HD]).astype(BF)
    n_qry = own.shape[0]
    own[...] = heads[where[0]]
    message[:n_qry] = heads[where[2]]
    message[n_qry:] = heads[where[3]]
    other[...] = heads[where[4]]


def output_kernel(where, begun, near, cross, w_out, out):
    def part(rows, head):
        return mm(rows[...], w_out[pl.ds(pl.multiple_of(head * HD, HD), HD)])

    out[...] = (begun[...] + part(near, where[2]) + part(cross, where[5])).astype(BF)


def whole(shape):
    return pl.BlockSpec(shape, lambda i, where: (0,) * len(shape))


def call(kernel, where, args, outs, scratch=()):
    return pl.pallas_call(
        kernel,
        out_shape=outs,
        grid_spec=pltpu.PrefetchScalarGridSpec(
            num_scalar_prefetch=1,
            grid=(1,),
            in_specs=[whole(a.shape) for a in args],
            out_specs=jax.tree.map(lambda o: whole(o.shape), outs),
            scratch_shapes=scratch,
        ),
        compiler_params=pltpu.CompilerParams(vmem_limit_bytes=32 << 20),
    )(where, *args)


def local(tokens, w_kv, w_rate, fast_weights, queries, w_query, out_gain, w_out):
    n_patch, n_view, n_head = (lax.axis_size(a) for a in ("patch", "view", "head"))
    patch, view, core = (lax.axis_index(a) for a in ("patch", "view", "head"))
    n_tok, width = tokens.shape
    n_qry = queries.shape[0]
    side = view % 2
    first = core == 0
    head = jnp.where(first, 2 * side, 1)
    sibling = jnp.where(first, 1, 2 * side)
    second = jnp.where(first, 1, 2 - 2 * side)
    where = jnp.stack([head, patch, sibling, second, 2 - 2 * side, 2 - 2 * side]).astype(jnp.int32)
    swap = [(0, 1), (1, 0)]

    def device(p, v, c):
        return (p * n_view + v) * n_head + c

    every = ("patch", "view", "head")
    ours = [(device(p, v, 0), device(p, v ^ 1, 0)) for p in range(n_patch) for v in range(n_view)]

    def rotate(n, shift):
        return [(i, (i + shift) % n) for i in range(n)]

    def pairs(s):
        return [(i, i ^ s) for i in range(n_patch)]

    far = [lax.ppermute(tokens, "view", rotate(n_view, s)) for s in range(1, n_view)]
    near = [tokens, lax.ppermute(tokens, "head", swap)]
    mine = lax.dynamic_index_in_dim(fast_weights, head, 2, keepdims=False).transpose(1, 0, 2)

    w_k = lax.dynamic_slice_in_dim(w_kv, head * HD, HD, 1)
    w_v = lax.dynamic_slice_in_dim(w_kv, width + head * HD, HD, 1)

    weights = [w_k, w_v, w_rate, mine]
    begun = call(
        functools.partial(first_kernel, len(near)),
        where,
        near + weights,
        jax.ShapeDtypeStruct((ROWS, HD), FP),
    )
    late, _ = lax.optimization_barrier((queries, begun))
    own_qry, message, other = call(
        query_kernel,
        where,
        [late, w_query],
        [jax.ShapeDtypeStruct((n, HD), BF) for n in (n_qry, 2 * n_qry, n_qry)],
        [pltpu.VMEM((HEADS, n_qry, HD), BF)],
    )
    begun, message, *far = lax.optimization_barrier((begun, message, *far))
    far = far + [lax.ppermute(f, "head", swap) for f in far]
    size = ROWS // n_patch
    chunks = call(
        functools.partial(second_kernel, len(far), n_patch),
        where,
        far + weights + [begun],
        [jax.ShapeDtypeStruct((size, HD), BF if s else FP) for s in range(n_patch)],
        [pltpu.VMEM((ROWS, HD), FP)],
    )
    rest = [*range(4, n_patch)]
    order = [2, 1, 3, *rest] if n_patch > 3 else [*range(1, n_patch)]
    order_back = [2, 1, 3, *rest] if n_patch > 3 else order
    got = {s: lax.ppermute(chunks[s], "patch", pairs(s)) for s in reversed(order)}
    own = chunks[0]
    for s in order:
        own = own + got[s].astype(FP)
    own = own.astype(BF)
    parts = {s: lax.ppermute(own, "patch", pairs(s)) for s in order_back}

    message, other, _ = lax.optimization_barrier((message, other, chunks[0]))
    swapped = lax.ppermute(message, "head", swap)
    across = lax.ppermute(jnp.concatenate([other, swapped[n_qry:]]), every, ours)

    gains = out_gain.reshape(1, width)
    normed, fresh = call(
        functools.partial(far_kernel, n_patch, order_back),
        where,
        [own] + [parts[s] for s in order_back] + [mine, gains, across],
        [jax.ShapeDtypeStruct((2 * n_qry, HD), BF), jax.ShapeDtypeStruct((3, FF, HD), BF)],
        [pltpu.VMEM((ROWS, HD), BF)],
    )
    back = lax.ppermute(normed, every, ours)
    for_other, begun = call(
        near_kernel,
        where,
        [own_qry, swapped[:n_qry], fresh, gains, w_out],
        [jax.ShapeDtypeStruct((n_qry, HD), BF), jax.ShapeDtypeStruct((n_qry, width), FP)],
    )
    near_out = lax.ppermute(for_other, "head", swap)
    begun, back = lax.optimization_barrier((begun, back))
    relayed = lax.ppermute(back[n_qry:], "head", swap)
    cross = jnp.where(first, back[:n_qry], relayed)
    return call(
        output_kernel,
        where,
        [begun, near_out, cross, w_out],
        jax.ShapeDtypeStruct((n_qry, width), BF),
    )


def solution(mesh):
    split = P(("groups", "patch", "view", "head"), None)
    in_specs = (split, P(), P(), P(), split, P(), P(), P())
    return jax.shard_map(local, mesh=mesh, in_specs=in_specs, out_specs=split, check_vma=False)
```

```python
import functools
import jax
import jax.numpy as jnp
from jax import lax
from jax.experimental import pallas as pl
from jax.experimental.pallas import tpu as pltpu
from jax.sharding import PartitionSpec as P

HEADS = 3
HD = 256
FF = 512
STEPS = 3

coef_a = 3.4445
coef_b = -4.775
coef_c = 2.0315
eta_rate = 3.0
eps_small = 1e-06

FP = jnp.float32
BF = jnp.bfloat16
NT = (((1,), (1,)), ((), ()))
TN = (((0,), (0,)), ((), ()))
ROWS = 3 * FF


def mm(a, b, dims=(((1,), (0,)), ((), ()))):
    return lax.dot_general(a, b, dims, preferred_element_type=FP)


def unit(raw):
    return raw * lax.rsqrt(jnp.sum(raw * raw, -1, keepdims=True) + eps_small)


def peer(index, shift):
    return index ^ shift


def add_gradient(tok, head, w_k, w_v, w_rate, fast, acc):
    rows = tok[...]
    keys = unit(mm(rows, w_k[...])).astype(BF)
    rates = mm(rows, w_rate[...], NT)
    pick = lax.broadcasted_iota(jnp.int32, rates.shape, 1) == head
    rate = jnp.sum(jnp.where(pick, rates, 0.0), -1, keepdims=True)
    rate = jnp.maximum(rate, 0.0) + jnp.log1p(jnp.exp(-jnp.abs(rate)))
    scaled = (rate * mm(rows, w_v[...])).astype(BF)
    gate_pre = mm(fast[0], keys, NT)
    up_pre = mm(fast[1], keys, NT)
    back = mm(fast[2], scaled, NT)
    sig = jax.nn.sigmoid(gate_pre)
    act = gate_pre * sig
    hidden = (act * up_pre).astype(BF)
    d_gate = (back * up_pre * sig * (1.0 + gate_pre * (1.0 - sig))).astype(BF)
    d_up = (back * act).astype(BF)
    acc[0:FF] += mm(d_gate, keys)
    acc[FF : 2 * FF] += mm(d_up, keys)
    acc[2 * FF : ROWS] += mm(hidden, scaled)


def first_kernel(n_tok, where, *refs):
    toks, (w_k, w_v, w_rate, fast, acc) = refs[:n_tok], refs[n_tok:]
    acc[...] = jnp.zeros_like(acc)
    for tok in toks:
        add_gradient(tok, where[0], w_k, w_v, w_rate, fast, acc)


def second_kernel(n_tok, n_patch, where, *refs):
    toks, (w_k, w_v, w_rate, fast, begun) = refs[:n_tok], refs[n_tok : n_tok + 5]
    outs, acc = refs[n_tok + 5 : -1], refs[-1]
    acc[...] = begun[...]
    for tok in toks:
        add_gradient(tok, where[0], w_k, w_v, w_rate, fast, acc)
    size = ROWS // n_patch
    for shift, out in enumerate(outs):
        chunk = peer(where[1], shift)
        out[...] = acc[pl.ds(pl.multiple_of(chunk * size, size), size)].astype(out.dtype)


def decode(rows, fresh, gain):
    gate_pre = mm(rows, fresh[0], NT)
    up_pre = mm(rows, fresh[1], NT)
    hidden = (gate_pre * jax.nn.sigmoid(gate_pre) * up_pre).astype(BF)
    read = mm(hidden, fresh[2])
    return (read * lax.rsqrt(jnp.mean(read * read, -1, keepdims=True) + eps_small) * gain).astype(BF)


def own_gain(gains, head):
    low, middle, high = (gains[:, i * HD : (i + 1) * HD] for i in range(HEADS))
    return jnp.where(head == 0, low, jnp.where(head == 1, middle, high)).astype(FP)


def near_kernel(where, own, fresh, gains, w_out, begun):
    gain = own_gain(gains, where[0])
    product = w_out[pl.ds(pl.multiple_of(where[0] * HD, HD), HD)]
    begun[...] = mm(decode(own[...], fresh, gain), product)


def far_kernel(n_patch, order, where, *refs):
    parts, (fast, gains, qry, other, *outs, fresh, grads) = refs[:n_patch], refs[n_patch:]
    size = ROWS // n_patch
    for shift, part in zip((0, *order), parts):
        chunk = peer(where[1], shift)
        grads[pl.ds(pl.multiple_of(chunk * size, size), size)] = part[...]
    ortho = []
    for kind in range(3):
        grad = grads[kind * FF : (kind + 1) * FF].astype(FP)
        total = jnp.sum(jnp.sum(grad * grad, -1, keepdims=True), 0, keepdims=True)
        ortho.append((grad / (jnp.sqrt(total) + eps_small)).astype(BF))
    for step in range(STEPS):
        gram = [mm(x, x, TN).astype(BF) for x in ortho]
        square = [mm(g, g) for g in gram]
        poly = [(coef_b * g.astype(FP) + coef_c * s).astype(BF) for g, s in zip(gram, square)]
        mixed = [mm(x, p) for x, p in zip(ortho, poly)]
        ortho = [(coef_a * x.astype(FP) + m).astype(BF) for x, m in zip(ortho, mixed)]
    for kind in range(3):
        old = fast[kind].astype(FP)
        moved = old + eta_rate * ortho[kind].astype(FP)
        old_norm = jnp.sqrt(jnp.sum(old * old, -1, keepdims=True))
        new_norm = jnp.sqrt(jnp.sum(moved * moved, -1, keepdims=True)) + eps_small
        fresh[kind] = (moved * (old_norm / new_norm)).astype(BF)
    gain = own_gain(gains, where[0])
    n_qry = other.shape[0]
    for i, out in enumerate(outs):
        out[...] = decode(qry[i * n_qry : (i + 1) * n_qry] if i < 2 else other[...], fresh, gain)


def query_kernel(where, queries, w_query, own, message, other, heads):
    rows = mm(queries[...], w_query[...])
    for head in range(HEADS):
        heads[head] = unit(rows[:, head * HD : (head + 1) * HD]).astype(BF)
    n_qry = own.shape[0]
    own[...] = heads[where[0]]
    message[:n_qry] = heads[where[2]]
    message[n_qry:] = heads[where[3]]
    other[...] = heads[where[4]]


def output_kernel(where, begun, near, to_first, to_second, w_out, out):
    def part(rows, head):
        return mm(rows, w_out[pl.ds(pl.multiple_of(head * HD, HD), HD)])

    cross = to_first[...] + to_second[...]
    out[...] = (begun[...] + part(near[...], where[2]) + part(cross, where[5])).astype(BF)


def whole(shape):
    return pl.BlockSpec(shape, lambda i, where: (0,) * len(shape))


def call(kernel, where, args, outs, scratch=()):
    return pl.pallas_call(
        kernel,
        out_shape=outs,
        grid_spec=pltpu.PrefetchScalarGridSpec(
            num_scalar_prefetch=1,
            grid=(1,),
            in_specs=[whole(a.shape) for a in args],
            out_specs=jax.tree.map(lambda o: whole(o.shape), outs),
            scratch_shapes=scratch,
        ),
        compiler_params=pltpu.CompilerParams(vmem_limit_bytes=32 << 20),
    )(where, *args)


def local(tokens, w_kv, w_rate, fast_weights, queries, w_query, out_gain, w_out):
    n_patch, n_view, n_head = (lax.axis_size(a) for a in ("patch", "view", "head"))
    patch, view, core = (lax.axis_index(a) for a in ("patch", "view", "head"))
    n_tok, width = tokens.shape
    n_qry = queries.shape[0]
    side = view % 2
    first = core == 0
    head = jnp.where(first, 2 * side, 1)
    sibling = jnp.where(first, 1, 2 * side)
    second = jnp.where(first, 1, 2 - 2 * side)
    where = jnp.stack([head, patch, sibling, second, 2 - 2 * side, 2 - 2 * side]).astype(jnp.int32)
    swap = [(0, 1), (1, 0)]

    def device(p, v, c):
        return (p * n_view + v) * n_head + c

    every = ("patch", "view", "head")
    ours = [(device(p, v, 0), device(p, v ^ 1, 0)) for p in range(n_patch) for v in range(n_view)]

    def rotate(n, shift):
        return [(i, (i + shift) % n) for i in range(n)]

    def pairs(s):
        return [(i, i ^ s) for i in range(n_patch)]

    far = [lax.ppermute(tokens, "view", rotate(n_view, s)) for s in range(1, n_view)]
    near = [tokens, lax.ppermute(tokens, "head", swap)]
    mine = lax.dynamic_index_in_dim(fast_weights, head, 2, keepdims=False).transpose(1, 0, 2)

    w_k = lax.dynamic_slice_in_dim(w_kv, head * HD, HD, 1)
    w_v = lax.dynamic_slice_in_dim(w_kv, width + head * HD, HD, 1)

    weights = [w_k, w_v, w_rate, mine]
    begun = call(
        functools.partial(first_kernel, len(near)),
        where,
        near + weights,
        jax.ShapeDtypeStruct((ROWS, HD), FP),
    )
    late, _ = lax.optimization_barrier((queries, begun))
    own_qry, message, other = call(
        query_kernel,
        where,
        [late, w_query],
        [jax.ShapeDtypeStruct((n, HD), BF) for n in (n_qry, 2 * n_qry, n_qry)],
        [pltpu.VMEM((HEADS, n_qry, HD), BF)],
    )
    begun, message, *far = lax.optimization_barrier((begun, message, *far))
    far = far + [lax.ppermute(f, "head", swap) for f in far]
    size = ROWS // n_patch
    chunks = call(
        functools.partial(second_kernel, len(far), n_patch),
        where,
        far + weights + [begun],
        [jax.ShapeDtypeStruct((size, HD), BF if s else FP) for s in range(n_patch)],
        [pltpu.VMEM((ROWS, HD), FP)],
    )
    rest = [*range(4, n_patch)]
    order = [2, 1, 3, *rest] if n_patch > 3 else [*range(1, n_patch)]
    order_back = [2, 1, 3, *rest] if n_patch > 3 else order
    got = {s: lax.ppermute(chunks[s], "patch", pairs(s)) for s in reversed(order)}
    own = chunks[0]
    for s in order:
        own = own + got[s].astype(FP)
    own = own.astype(BF)
    parts = {s: lax.ppermute(own, "patch", pairs(s)) for s in order_back}

    message, other, _ = lax.optimization_barrier((message, other, chunks[0]))
    swapped = lax.ppermute(message, "head", swap)
    across = lax.ppermute(jnp.concatenate([other, swapped[n_qry:]]), every, ours)

    gains = out_gain.reshape(1, width)
    for_first, for_second, for_other, fresh = call(
        functools.partial(far_kernel, n_patch, order_back),
        where,
        [own] + [parts[s] for s in order_back] + [mine, gains, across, swapped[:n_qry]],
        [jax.ShapeDtypeStruct((n_qry, HD), BF)] * 3 + [jax.ShapeDtypeStruct((3, FF, HD), BF)],
        [pltpu.VMEM((ROWS, HD), BF)],
    )
    to_first = lax.ppermute(for_first, every, ours)
    to_second = lax.ppermute(for_second, every, [(a, b + 1) for a, b in ours])
    near_out = lax.ppermute(for_other, "head", swap)
    begun = call(
        near_kernel,
        where,
        [own_qry, fresh, gains, w_out],
        jax.ShapeDtypeStruct((n_qry, width), FP),
    )
    return call(
        output_kernel,
        where,
        [begun, near_out, to_first, to_second, w_out],
        jax.ShapeDtypeStruct((n_qry, width), BF),
    )


def solution(mesh):
    split = P(("groups", "patch", "view", "head"), None)
    in_specs = (split, P(), P(), P(), split, P(), P(), P())
    return jax.shard_map(local, mesh=mesh, in_specs=in_specs, out_specs=split, check_vma=False)
```

```python
import functools
import jax
import jax.numpy as jnp
from jax import lax
from jax.experimental import pallas as pl
from jax.experimental.pallas import tpu as pltpu
from jax.sharding import PartitionSpec as P

HEADS = 3
HD = 256
FF = 512
STEPS = 3

coef_a = 3.4445
coef_b = -4.775
coef_c = 2.0315
eta_rate = 3.0
eps_small = 1e-06

FP = jnp.float32
BF = jnp.bfloat16
NT = (((1,), (1,)), ((), ()))
TN = (((0,), (0,)), ((), ()))
LARGE = FF // 2
SMALL = FF // 4


def exchange_order(n_patch):
    return [0, 2, 1, 3, *range(4, n_patch)] if n_patch > 3 else [*range(n_patch)]


def mm(a, b, dims=(((1,), (0,)), ((), ()))):
    return lax.dot_general(a, b, dims, preferred_element_type=FP)


def unit(raw):
    return raw * lax.rsqrt(jnp.sum(raw * raw, -1, keepdims=True) + eps_small)


def add_gradient(rows, segment, acc):
    head, w_k, w_v, w_rate, fast = segment
    keys = unit(mm(rows, w_k[...])).astype(BF)
    rates = mm(rows, w_rate[...], NT)
    pick = lax.broadcasted_iota(jnp.int32, rates.shape, 1) == head
    rate = jnp.sum(jnp.where(pick, rates, 0.0), -1, keepdims=True)
    rate = jnp.maximum(rate, 0.0) + jnp.log1p(jnp.exp(-jnp.abs(rate)))
    scaled = (rate * mm(rows, w_v[...])).astype(BF)
    gate_pre = mm(fast[0], keys, NT)
    up_pre = mm(fast[1], keys, NT)
    back = mm(fast[2], scaled, NT)
    sig = jax.nn.sigmoid(gate_pre)
    act = gate_pre * sig
    hidden = (act * up_pre).astype(BF)
    d_gate = (back * up_pre * sig * (1.0 + gate_pre * (1.0 - sig))).astype(BF)
    d_up = (back * act).astype(BF)
    acc[0] += mm(d_gate, keys)
    acc[1] += mm(d_up, keys)
    acc[2] += mm(hidden, scaled)


def add_segments(where, toks, weights, accs):
    w_rate, *weights = weights
    for i, acc in enumerate(accs):
        w_k, w_v, fast = weights[3 * i : 3 * i + 3]
        for tok in toks:
            for at in range(0, tok.shape[0], HD):
                add_gradient(tok[at : at + HD], (where[6 + i], w_k, w_v, w_rate, fast), acc)


def first_kernel(n_tok, where, *refs):
    toks, weights, accs = refs[:n_tok], refs[n_tok:-2], refs[-2:]
    for acc in accs:
        acc[...] = jnp.zeros_like(acc)
    add_segments(where, toks, weights, accs)


def second_kernel(n_tok, n_patch, where, *refs):
    toks, weights, begun = refs[:n_tok], refs[n_tok : n_tok + 7], refs[n_tok + 7 : n_tok + 9]
    outs, accs = refs[n_tok + 9 : -2], refs[-2:]
    for acc, part in zip(accs, begun):
        acc[...] = part[...]
    add_segments(where, toks, weights, accs)
    for out, shift in zip(outs, exchange_order(n_patch)):
        chunk = where[1] ^ shift
        at = 0
        for acc in accs:
            size = acc.shape[1] // n_patch
            out[:, at : at + size] = acc[:, pl.ds(pl.multiple_of(chunk * size, size), size)].astype(out.dtype)
            at += size


def collect_kernel(n_patch, where, *refs):
    parts, segments = refs[:n_patch], refs[n_patch:]
    for part, shift in zip(parts, exchange_order(n_patch)):
        chunk = where[1] ^ shift
        at = 0
        for segment in segments:
            size = segment.shape[1] // n_patch
            segment[:, pl.ds(pl.multiple_of(chunk * size, size), size)] = part[:, at : at + size]
            at += size


def decode(rows, fresh, gain):
    gate_pre = mm(rows, fresh[0], NT)
    up_pre = mm(rows, fresh[1], NT)
    hidden = (gate_pre * jax.nn.sigmoid(gate_pre) * up_pre).astype(BF)
    read = mm(hidden, fresh[2])
    return (read * lax.rsqrt(jnp.mean(read * read, -1, keepdims=True) + eps_small) * gain).astype(BF)


def own_gain(gains, head):
    low, middle, high = (gains[:, i * HD : (i + 1) * HD] for i in range(HEADS))
    return jnp.where(head == 0, low, jnp.where(head == 1, middle, high)).astype(FP)


def near_kernel(where, own, other, fresh, gains, w_out, for_other, begun):
    gain = own_gain(gains, where[0])
    for_other[...] = decode(other[...], fresh, gain)
    product = w_out[pl.ds(pl.multiple_of(where[0] * HD, HD), HD)]
    begun[...] = mm(decode(own[...], fresh, gain), product)


def far_kernel(where, large, small, rest, half, fast, gains, qry, out, fresh, grads):
    @pl.when(where[8] == 0)
    def _():
        grads[:, :LARGE] = large[...]
        grads[:, LARGE : LARGE + SMALL] = small[...]
        grads[:, LARGE + SMALL :] = rest[...]

    @pl.when(where[8] == 1)
    def _():
        at = pl.multiple_of(where[9] * LARGE, LARGE)
        grads[:, pl.ds(at, LARGE)] = large[...]
        grads[:, pl.ds(pl.multiple_of(LARGE - at, LARGE), LARGE)] = half[...]

    ortho = []
    for kind in range(3):
        grad = grads[kind].astype(FP)
        total = jnp.sum(jnp.sum(grad * grad, -1, keepdims=True), 0, keepdims=True)
        ortho.append((grad / (jnp.sqrt(total) + eps_small)).astype(BF))
    for step in range(STEPS):
        gram = [mm(x, x, TN).astype(BF) for x in ortho]
        square = [mm(g, g) for g in gram]
        poly = [(coef_b * g.astype(FP) + coef_c * s).astype(BF) for g, s in zip(gram, square)]
        mixed = [mm(x, p) for x, p in zip(ortho, poly)]
        ortho = [(coef_a * x.astype(FP) + m).astype(BF) for x, m in zip(ortho, mixed)]
    for kind in range(3):
        old = fast[kind].astype(FP)
        moved = old + eta_rate * ortho[kind].astype(FP)
        old_norm = jnp.sqrt(jnp.sum(old * old, -1, keepdims=True))
        new_norm = jnp.sqrt(jnp.sum(moved * moved, -1, keepdims=True)) + eps_small
        fresh[kind] = (moved * (old_norm / new_norm)).astype(BF)
    gain = own_gain(gains, where[0])

    @pl.when(where[8] == 0)
    def _():
        for row in range(0, qry.shape[0], HD):
            out[row : row + HD] = decode(qry[row : row + HD], fresh, gain)


def query_kernel(where, queries, w_query, own, message, other, heads):
    rows = mm(queries[...], w_query[...])
    for head in range(HEADS):
        heads[head] = unit(rows[:, head * HD : (head + 1) * HD]).astype(BF)
    n_qry = own.shape[0]
    own[...] = heads[where[0]]
    message[:n_qry] = heads[where[2]]
    message[n_qry:] = heads[where[3]]
    other[...] = heads[where[4]]


def output_kernel(where, begun, near, back, relayed, w_out, out):
    def part(rows, head):
        return mm(rows, w_out[pl.ds(pl.multiple_of(head * HD, HD), HD)])

    cross = jnp.where(where[8] == 0, back[: relayed.shape[0]], relayed[...])
    out[...] = (begun[...] + part(near[...], where[2]) + part(cross, where[5])).astype(BF)


def whole(shape):
    return pl.BlockSpec(shape, lambda i, where: (0,) * len(shape))


def call(kernel, where, args, outs, scratch=()):
    return pl.pallas_call(
        kernel,
        out_shape=outs,
        grid_spec=pltpu.PrefetchScalarGridSpec(
            num_scalar_prefetch=1,
            grid=(1,),
            in_specs=[whole(a.shape) for a in args],
            out_specs=jax.tree.map(lambda o: whole(o.shape), outs),
            scratch_shapes=scratch,
        ),
        compiler_params=pltpu.CompilerParams(vmem_limit_bytes=32 << 20),
    )(where, *args)


def local(tokens, w_kv, w_rate, fast_weights, queries, w_query, out_gain, w_out):
    n_patch, n_view, n_head = (lax.axis_size(a) for a in ("patch", "view", "head"))
    patch, view, core = (lax.axis_index(a) for a in ("patch", "view", "head"))
    n_tok, width = tokens.shape
    n_qry = queries.shape[0]
    side = view % 2
    first = core == 0
    head = jnp.where(first, 2 * side, 1)
    sibling = jnp.where(first, 1, 2 * side)
    second = jnp.where(first, 1, 2 - 2 * side)
    units = jnp.where(first, 0, side * LARGE), jnp.where(first, LARGE, LARGE + SMALL)
    where = [head, patch, sibling, second, 2 - 2 * side, 2 - 2 * side, head, 2 * side, core, side]
    where = jnp.stack(where).astype(jnp.int32)
    swap = [(0, 1), (1, 0)]

    def device(p, v, c):
        return (p * n_view + v) * n_head + c

    every = ("patch", "view", "head")
    ours = [(device(p, v, 0), device(p, v ^ 1, 0)) for p in range(n_patch) for v in range(n_view)]

    def rotate(n, shift):
        return [(i, (i + shift) % n) for i in range(n)]

    seconds = [(a + 1, b + 1) for a, b in ours]

    def pairs(s):
        return [(i, i ^ s) for i in range(n_patch)]

    far = [lax.ppermute(tokens, "view", rotate(n_view, s)) for s in range(1, n_view)]
    near = [tokens, lax.ppermute(tokens, "head", swap)]
    mine = lax.dynamic_index_in_dim(fast_weights, head, 2, keepdims=False).transpose(1, 0, 2)

    weights = [w_rate]
    for owner, unit_at, size in ((head, units[0], LARGE), (2 * side, units[1], SMALL)):
        weights.append(lax.dynamic_slice_in_dim(w_kv, owner * HD, HD, 1))
        weights.append(lax.dynamic_slice_in_dim(w_kv, width + owner * HD, HD, 1))
        piece = lax.dynamic_slice(fast_weights, (unit_at, 0, owner, 0), (size, 3, 1, HD))
        weights.append(piece.reshape(size, 3, HD).transpose(1, 0, 2))
    sums = [jax.ShapeDtypeStruct((3, size, HD), FP) for size in (LARGE, SMALL)]
    begun = list(call(functools.partial(first_kernel, len(near)), where, near + weights, sums))
    late, _ = lax.optimization_barrier((queries, begun[0]))
    own_qry, message, other = call(
        query_kernel,
        where,
        [late, w_query],
        [jax.ShapeDtypeStruct((n, HD), BF) for n in (n_qry, 2 * n_qry, n_qry)],
        [pltpu.VMEM((HEADS, n_qry, HD), BF)],
    )
    begun[0], message, *far = lax.optimization_barrier((begun[0], message, *far))
    far = far + [lax.ppermute(f, "head", swap) for f in far]
    size = (LARGE + SMALL) // n_patch
    chunks = call(
        functools.partial(second_kernel, len(far), n_patch),
        where,
        far + weights + begun,
        [jax.ShapeDtypeStruct((3, size, HD), BF if k else FP) for k in range(n_patch)],
        [pltpu.VMEM(s.shape, FP) for s in sums],
    )
    order = exchange_order(n_patch)
    got = [lax.ppermute(chunks[k], "patch", pairs(order[k])) for k in range(n_patch - 1, 0, -1)]
    own = chunks[0]
    for part in got:
        own = own + part.astype(FP)
    own = own.astype(BF)
    parts = [lax.ppermute(own, "patch", pairs(s)) for s in exchange_order(n_patch)[1:]]

    message, other, _ = lax.optimization_barrier((message, other, chunks[0]))
    swapped = lax.ppermute(message, "head", swap)
    across = lax.ppermute(jnp.concatenate([other, swapped[n_qry:]]), every, ours)

    large, small = call(
        functools.partial(collect_kernel, n_patch),
        where,
        [own, *parts],
        [jax.ShapeDtypeStruct(s.shape, BF) for s in sums],
    )
    rest = lax.ppermute(small, "head", swap)
    half = lax.ppermute(large, every, seconds)
    gains = out_gain.reshape(1, width)
    normed, fresh = call(
        far_kernel,
        where,
        [large, small, rest, half, mine, gains, across],
        [jax.ShapeDtypeStruct((2 * n_qry, HD), BF), jax.ShapeDtypeStruct((3, FF, HD), BF)],
        [pltpu.VMEM((3, FF, HD), BF)],
    )
    back = lax.ppermute(normed, every, ours)
    for_other, begun = call(
        near_kernel,
        where,
        [own_qry, swapped[:n_qry], fresh, gains, w_out],
        [jax.ShapeDtypeStruct((n_qry, HD), BF), jax.ShapeDtypeStruct((n_qry, width), FP)],
    )
    near_out = lax.ppermute(for_other, "head", swap)
    begun, back = lax.optimization_barrier((begun, back))
    relayed = lax.ppermute(back[n_qry:], "head", swap)
    return call(
        output_kernel,
        where,
        [begun, near_out, back, relayed, w_out],
        jax.ShapeDtypeStruct((n_qry, width), BF),
    )


def solution(mesh):
    split = P(("groups", "patch", "view", "head"), None)
    in_specs = (split, P(), P(), P(), split, P(), P(), P())
    return jax.shard_map(local, mesh=mesh, in_specs=in_specs, out_specs=split, check_vma=False)
```

```python
import functools
import jax
import jax.numpy as jnp
from jax import lax
from jax.experimental import pallas as pl
from jax.experimental.pallas import tpu as pltpu
from jax.sharding import PartitionSpec as P

HEADS = 3
HD = 256
FF = 512
STEPS = 3

coef_a = 3.4445
coef_b = -4.775
coef_c = 2.0315
eta_rate = 3.0
eps_small = 1e-06

FP = jnp.float32
BF = jnp.bfloat16
NT = (((1,), (1,)), ((), ()))
TN = (((0,), (0,)), ((), ()))
LARGE = FF // 2
SMALL = FF // 4


def exchange_order(n_patch, back=False):
    if n_patch < 4:
        return [*range(n_patch)]
    return [0, *((2, 1, 3) if back else (3, 1, 2)), *range(4, n_patch)]


def mm(a, b, dims=(((1,), (0,)), ((), ()))):
    return lax.dot_general(a, b, dims, preferred_element_type=FP)


def unit(raw):
    return raw * lax.rsqrt(jnp.sum(raw * raw, -1, keepdims=True) + eps_small)


def project(rows, head, w_k, w_v, w_rate, keys, scaled):
    keys[...] = unit(mm(rows, w_k[...])).astype(BF)
    rates = mm(rows, w_rate[...], NT)
    pick = lax.broadcasted_iota(jnp.int32, rates.shape, 1) == head
    rate = jnp.sum(jnp.where(pick, rates, 0.0), -1, keepdims=True)
    rate = jnp.maximum(rate, 0.0) + jnp.log1p(jnp.exp(-jnp.abs(rate)))
    scaled[...] = (rate * mm(rows, w_v[...])).astype(BF)


def add_gradient(keys, scaled, fast, acc):
    gate_pre = mm(fast[0], keys, NT)
    up_pre = mm(fast[1], keys, NT)
    back = mm(fast[2], scaled, NT)
    sig = jax.nn.sigmoid(gate_pre)
    act = gate_pre * sig
    hidden = (act * up_pre).astype(BF)
    d_gate = (back * up_pre * sig * (1.0 + gate_pre * (1.0 - sig))).astype(BF)
    d_up = (back * act).astype(BF)
    acc[0] += mm(d_gate, keys)
    acc[1] += mm(d_up, keys)
    acc[2] += mm(hidden, scaled)


def add_segments(where, toks, weights, accs, keys, scaled):
    w_rate, *weights = weights
    large, small = weights[:3], weights[3:]
    both = [(tok, at) for tok in toks for at in range(0, tok.shape[0], HD)]
    for i, (tok, at) in enumerate(both):
        rows = tok[at : at + HD]
        project(rows, where[6], *large[:2], w_rate, keys.at[i], scaled.at[i])
        add_gradient(keys[i], scaled[i], large[2], accs[0])

    @pl.when(where[8] != 0)
    def _():
        for i, (tok, at) in enumerate(both):
            project(tok[at : at + HD], where[7], *small[:2], w_rate, keys.at[i], scaled.at[i])

    for i in range(len(both)):
        add_gradient(keys[i], scaled[i], small[2], accs[1])


def first_kernel(n_tok, where, *refs):
    toks, weights, accs, rows = refs[:n_tok], refs[n_tok:-4], refs[-4:-2], refs[-2:]
    for acc in accs:
        acc[...] = jnp.zeros_like(acc)
    add_segments(where, toks, weights, accs, *rows)


def second_kernel(n_tok, n_patch, where, *refs):
    toks, weights, begun = refs[:n_tok], refs[n_tok : n_tok + 7], refs[n_tok + 7 : n_tok + 9]
    outs, accs, rows = refs[n_tok + 9 : -4], refs[-4:-2], refs[-2:]
    for acc, part in zip(accs, begun):
        acc[...] = part[...]
    add_segments(where, toks, weights, accs, *rows)
    for out, shift in zip(outs, exchange_order(n_patch)):
        chunk = where[1] ^ shift
        at = 0
        for acc in accs:
            size = acc.shape[1] // n_patch
            out[:, at : at + size] = acc[:, pl.ds(pl.multiple_of(chunk * size, size), size)].astype(out.dtype)
            at += size


def collect_kernel(n_patch, where, *refs):
    parts, segments = refs[:n_patch], refs[n_patch:]
    for part, shift in zip(parts, exchange_order(n_patch, True)):
        chunk = where[1] ^ shift
        at = 0
        for segment in segments:
            size = segment.shape[1] // n_patch
            segment[:, pl.ds(pl.multiple_of(chunk * size, size), size)] = part[:, at : at + size]
            at += size


def decode(rows, fresh, gain):
    gate_pre = mm(rows, fresh[0], NT)
    up_pre = mm(rows, fresh[1], NT)
    hidden = (gate_pre * jax.nn.sigmoid(gate_pre) * up_pre).astype(BF)
    read = mm(hidden, fresh[2])
    return (read * lax.rsqrt(jnp.mean(read * read, -1, keepdims=True) + eps_small) * gain).astype(BF)


def own_gain(gains, head):
    low, middle, high = (gains[:, i * HD : (i + 1) * HD] for i in range(HEADS))
    return jnp.where(head == 0, low, jnp.where(head == 1, middle, high)).astype(FP)


def near_kernel(where, own, other, fresh, gains, w_out, for_other, begun):
    gain = own_gain(gains, where[0])
    for_other[...] = decode(other[...], fresh, gain)
    product = w_out[pl.ds(pl.multiple_of(where[0] * HD, HD), HD)]
    begun[...] = mm(decode(own[...], fresh, gain), product)


def far_kernel(where, large, small, rest, half, fast, gains, qry, out, fresh, grads):
    @pl.when(where[8] == 0)
    def _():
        grads[:, :LARGE] = large[...]
        grads[:, LARGE : LARGE + SMALL] = small[...]
        grads[:, LARGE + SMALL :] = rest[...]

    @pl.when(where[8] == 1)
    def _():
        at = pl.multiple_of(where[9] * LARGE, LARGE)
        grads[:, pl.ds(at, LARGE)] = large[...]
        grads[:, pl.ds(pl.multiple_of(LARGE - at, LARGE), LARGE)] = half[...]

    ortho = []
    for kind in range(3):
        grad = grads[kind].astype(FP)
        total = jnp.sum(jnp.sum(grad * grad, -1, keepdims=True), 0, keepdims=True)
        ortho.append((grad / (jnp.sqrt(total) + eps_small)).astype(BF))
    for step in range(STEPS):
        gram = [mm(x, x, TN).astype(BF) for x in ortho]
        square = [mm(g, g) for g in gram]
        poly = [(coef_b * g.astype(FP) + coef_c * s).astype(BF) for g, s in zip(gram, square)]
        mixed = [mm(x, p) for x, p in zip(ortho, poly)]
        ortho = [(coef_a * x.astype(FP) + m).astype(BF) for x, m in zip(ortho, mixed)]
    for kind in range(3):
        old = fast[kind].astype(FP)
        moved = old + eta_rate * ortho[kind].astype(FP)
        old_norm = jnp.sqrt(jnp.sum(old * old, -1, keepdims=True))
        new_norm = jnp.sqrt(jnp.sum(moved * moved, -1, keepdims=True)) + eps_small
        fresh[kind] = (moved * (old_norm / new_norm)).astype(BF)
    gain = own_gain(gains, where[0])

    @pl.when(where[8] == 0)
    def _():
        for row in range(0, qry.shape[0], HD):
            out[row : row + HD] = decode(qry[row : row + HD], fresh, gain)


def query_kernel(where, queries, w_query, own, message, other, heads):
    rows = mm(queries[...], w_query[...])
    for head in range(HEADS):
        heads[head] = unit(rows[:, head * HD : (head + 1) * HD]).astype(BF)
    n_qry = own.shape[0]
    own[...] = heads[where[0]]
    message[:n_qry] = heads[where[2]]
    message[n_qry:] = heads[where[3]]
    other[...] = heads[where[4]]


def output_kernel(where, begun, near, back, relayed, w_out, out):
    def part(rows, head):
        return mm(rows, w_out[pl.ds(pl.multiple_of(head * HD, HD), HD)])

    cross = jnp.where(where[8] == 0, back[: relayed.shape[0]], relayed[...])
    out[...] = (begun[...] + part(near[...], where[2]) + part(cross, where[5])).astype(BF)


def whole(shape):
    return pl.BlockSpec(shape, lambda i, where: (0,) * len(shape))


def call(kernel, where, args, outs, scratch=()):
    return pl.pallas_call(
        kernel,
        out_shape=outs,
        grid_spec=pltpu.PrefetchScalarGridSpec(
            num_scalar_prefetch=1,
            grid=(1,),
            in_specs=[whole(a.shape) for a in args],
            out_specs=jax.tree.map(lambda o: whole(o.shape), outs),
            scratch_shapes=scratch,
        ),
        compiler_params=pltpu.CompilerParams(vmem_limit_bytes=32 << 20),
    )(where, *args)


def local(tokens, w_kv, w_rate, fast_weights, queries, w_query, out_gain, w_out):
    n_patch, n_view, n_head = (lax.axis_size(a) for a in ("patch", "view", "head"))
    patch, view, core = (lax.axis_index(a) for a in ("patch", "view", "head"))
    n_tok, width = tokens.shape
    n_qry = queries.shape[0]
    side = view % 2
    first = core == 0
    head = jnp.where(first, 2 * side, 1)
    sibling = jnp.where(first, 1, 2 * side)
    second = jnp.where(first, 1, 2 - 2 * side)
    units = jnp.where(first, 0, side * LARGE), jnp.where(first, LARGE, LARGE + SMALL)
    where = [head, patch, sibling, second, 2 - 2 * side, 2 - 2 * side, head, 2 * side, core, side]
    where = jnp.stack(where).astype(jnp.int32)
    swap = [(0, 1), (1, 0)]

    def device(p, v, c):
        return (p * n_view + v) * n_head + c

    every = ("patch", "view", "head")
    ours = [(device(p, v, 0), device(p, v ^ 1, 0)) for p in range(n_patch) for v in range(n_view)]

    def rotate(n, shift):
        return [(i, (i + shift) % n) for i in range(n)]

    seconds = [(a + 1, b + 1) for a, b in ours]

    def pairs(s):
        return [(i, i ^ s) for i in range(n_patch)]

    far = [lax.ppermute(tokens, "view", rotate(n_view, s)) for s in range(1, n_view)]
    near = [tokens, lax.ppermute(tokens, "head", swap)]
    mine = lax.dynamic_index_in_dim(fast_weights, head, 2, keepdims=False).transpose(1, 0, 2)

    weights = [w_rate]
    for owner, unit_at, size in ((head, units[0], LARGE), (2 * side, units[1], SMALL)):
        weights.append(lax.dynamic_slice_in_dim(w_kv, owner * HD, HD, 1))
        weights.append(lax.dynamic_slice_in_dim(w_kv, width + owner * HD, HD, 1))
        piece = lax.dynamic_slice(fast_weights, (unit_at, 0, owner, 0), (size, 3, 1, HD))
        weights.append(piece.reshape(size, 3, HD).transpose(1, 0, 2))
    sums = [jax.ShapeDtypeStruct((3, size, HD), FP) for size in (LARGE, SMALL)]

    def held(toks):
        return [pltpu.VMEM((len(toks) * n_tok // HD, HD, HD), BF)] * 2

    begun = list(call(functools.partial(first_kernel, len(near)), where, near + weights, sums, held(near)))
    late, _ = lax.optimization_barrier((queries, begun[0]))
    own_qry, message, other = call(
        query_kernel,
        where,
        [late, w_query],
        [jax.ShapeDtypeStruct((n, HD), BF) for n in (n_qry, 2 * n_qry, n_qry)],
        [pltpu.VMEM((HEADS, n_qry, HD), BF)],
    )
    begun[0], message, *far = lax.optimization_barrier((begun[0], message, *far))
    far = far + [lax.ppermute(f, "head", swap) for f in far]
    message, far[-1] = lax.optimization_barrier((message, far[-1]))
    swapped = lax.ppermute(message, "head", swap)
    size = (LARGE + SMALL) // n_patch
    chunks = call(
        functools.partial(second_kernel, len(far), n_patch),
        where,
        far + weights + begun,
        [jax.ShapeDtypeStruct((3, size, HD), BF if k else FP) for k in range(n_patch)],
        [pltpu.VMEM(s.shape, FP) for s in sums] + held(far),
    )
    order = exchange_order(n_patch)
    got = [lax.ppermute(chunks[k], "patch", pairs(order[k])) for k in range(n_patch - 1, 0, -1)]
    own = chunks[0]
    for part in got:
        own = own + part.astype(FP)
    other, swapped, _ = lax.optimization_barrier((other, swapped, chunks[0]))
    across = lax.ppermute(jnp.concatenate([other, swapped[n_qry:]]), every, ours)
    own = own.astype(BF)
    parts = [lax.ppermute(own, "patch", pairs(s)) for s in exchange_order(n_patch, True)[1:]]
    parts[0], across = lax.optimization_barrier((parts[0], across))
    large, small = call(
        functools.partial(collect_kernel, n_patch),
        where,
        [own, *parts],
        [jax.ShapeDtypeStruct(s.shape, BF) for s in sums],
    )
    rest = lax.ppermute(small, "head", swap)
    large, rest = lax.optimization_barrier((large, rest))
    half = lax.ppermute(large, every, seconds)
    gains = out_gain.reshape(1, width)
    normed, fresh = call(
        far_kernel,
        where,
        [large, small, rest, half, mine, gains, across],
        [jax.ShapeDtypeStruct((2 * n_qry, HD), BF), jax.ShapeDtypeStruct((3, FF, HD), BF)],
        [pltpu.VMEM((3, FF, HD), BF)],
    )
    back = lax.ppermute(normed, every, ours)
    for_other, begun = call(
        near_kernel,
        where,
        [own_qry, swapped[:n_qry], fresh, gains, w_out],
        [jax.ShapeDtypeStruct((n_qry, HD), BF), jax.ShapeDtypeStruct((n_qry, width), FP)],
    )
    near_out = lax.ppermute(for_other, "head", swap)
    begun, back = lax.optimization_barrier((begun, back))
    relayed = lax.ppermute(back[n_qry:], "head", swap)
    return call(
        output_kernel,
        where,
        [begun, near_out, back, relayed, w_out],
        jax.ShapeDtypeStruct((n_qry, width), BF),
    )


def solution(mesh):
    split = P(("groups", "patch", "view", "head"), None)
    in_specs = (split, P(), P(), P(), split, P(), P(), P())
    return jax.shard_map(local, mesh=mesh, in_specs=in_specs, out_specs=split, check_vma=False)
```

```python
import functools
import jax
import jax.numpy as jnp
from jax import lax
from jax.experimental import pallas as pl
from jax.experimental.pallas import tpu as pltpu
from jax.sharding import PartitionSpec as P

HEADS = 3
HD = 256
FF = 512
STEPS = 3

coef_a = 3.4445
coef_b = -4.775
coef_c = 2.0315
eta_rate = 3.0
eps_small = 1e-06

FP = jnp.float32
BF = jnp.bfloat16
NT = (((1,), (1,)), ((), ()))
TN = (((0,), (0,)), ((), ()))
LARGE = FF // 2
SMALL = FF // 4


def exchange_order(n_patch, back=False):
    if n_patch < 4:
        return [*range(n_patch)]
    return [0, *((2, 1, 3) if back else (3, 1, 2)), *range(4, n_patch)]


def mm(a, b, dims=(((1,), (0,)), ((), ()))):
    return lax.dot_general(a, b, dims, preferred_element_type=FP)


def unit(raw):
    return raw * lax.rsqrt(jnp.sum(raw * raw, -1, keepdims=True) + eps_small)


def project(rows, head, w_k, w_v, w_rate, keys, scaled):
    keys[...] = unit(mm(rows, w_k[...])).astype(BF)
    rates = mm(rows, w_rate[...], NT)
    pick = lax.broadcasted_iota(jnp.int32, rates.shape, 1) == head
    rate = jnp.sum(jnp.where(pick, rates, 0.0), -1, keepdims=True)
    rate = jnp.maximum(rate, 0.0) + jnp.log1p(jnp.exp(-jnp.abs(rate)))
    scaled[...] = (rate * mm(rows, w_v[...])).astype(BF)


def gradient(keys, scaled, fast, begun, acc):
    gate_pre = mm(fast[0], keys, NT)
    up_pre = mm(fast[1], keys, NT)
    back = mm(fast[2], scaled, NT)
    sig = jax.nn.sigmoid(gate_pre)
    act = gate_pre * sig
    hidden = (act * up_pre).astype(BF)
    d_gate = (back * up_pre * sig * (1.0 + gate_pre * (1.0 - sig))).astype(BF)
    d_up = (back * act).astype(BF)
    for kind, (left, right) in enumerate(((d_gate, keys), (d_up, keys), (hidden, scaled))):
        product = mm(left, right)
        acc[kind] = product if begun is None else begun[kind] + product


def segments(where, toks, weights, begun, accs, keys, scaled):
    w_rate, *weights = weights
    large, small = weights[:3], weights[3:]
    rows = jnp.concatenate([tok[...] for tok in toks])
    project(rows, where[6], *large[:2], w_rate, keys, scaled)
    gradient(keys[...], scaled[...], large[2], begun[0], accs[0])

    @pl.when(where[8] != 0)
    def _():
        project(rows, where[7], *small[:2], w_rate, keys, scaled)

    gradient(keys[...], scaled[...], small[2], begun[1], accs[1])


def first_kernel(n_tok, where, *refs):
    toks, weights, accs, rows = refs[:n_tok], refs[n_tok:-4], refs[-4:-2], refs[-2:]
    segments(where, toks, weights, (None, None), accs, *rows)


def second_kernel(n_tok, n_patch, where, *refs):
    toks, weights, begun = refs[:n_tok], refs[n_tok : n_tok + 7], refs[n_tok + 7 : n_tok + 9]
    outs, accs, rows = refs[n_tok + 9 : -4], refs[-4:-2], refs[-2:]
    segments(where, toks, weights, begun, accs, *rows)
    for out, shift in zip(outs, exchange_order(n_patch)):
        chunk = where[1] ^ shift
        at = 0
        for acc in accs:
            size = acc.shape[1] // n_patch
            out[:, at : at + size] = acc[:, pl.ds(pl.multiple_of(chunk * size, size), size)].astype(out.dtype)
            at += size


def collect_kernel(n_patch, where, *refs):
    parts, pieces = refs[:n_patch], refs[n_patch:]
    for part, shift in zip(parts, exchange_order(n_patch, True)):
        chunk = where[1] ^ shift
        at = 0
        for piece in pieces:
            size = piece.shape[1] // n_patch
            piece[:, pl.ds(pl.multiple_of(chunk * size, size), size)] = part[:, at : at + size]
            at += size


def decode(rows, fresh, gain):
    gate_pre = mm(rows, fresh[0], NT)
    up_pre = mm(rows, fresh[1], NT)
    hidden = (gate_pre * jax.nn.sigmoid(gate_pre) * up_pre).astype(BF)
    read = mm(hidden, fresh[2])
    return (read * lax.rsqrt(jnp.mean(read * read, -1, keepdims=True) + eps_small) * gain).astype(BF)


def own_gain(gains, head):
    low, middle, high = (gains[:, i * HD : (i + 1) * HD] for i in range(HEADS))
    return jnp.where(head == 0, low, jnp.where(head == 1, middle, high)).astype(FP)


def near_kernel(where, own, other, fresh, gains, w_out, for_other, begun):
    gain = own_gain(gains, where[0])
    for_other[...] = decode(other[...], fresh, gain)
    product = w_out[pl.ds(pl.multiple_of(where[0] * HD, HD), HD)]
    begun[...] = mm(decode(own[...], fresh, gain), product)


def far_kernel(where, large, small, rest, half, fast, gains, qry, out, fresh, grads):
    @pl.when(where[8] == 0)
    def _():
        grads[:, :LARGE] = large[...]
        grads[:, LARGE : LARGE + SMALL] = small[...]
        grads[:, LARGE + SMALL :] = rest[...]

    @pl.when(where[8] == 1)
    def _():
        at = pl.multiple_of(where[9] * LARGE, LARGE)
        grads[:, pl.ds(at, LARGE)] = large[...]
        grads[:, pl.ds(pl.multiple_of(LARGE - at, LARGE), LARGE)] = half[...]

    ortho = []
    for kind in range(3):
        grad = grads[kind].astype(FP)
        total = jnp.sum(jnp.sum(grad * grad, -1, keepdims=True), 0, keepdims=True)
        ortho.append((grad / (jnp.sqrt(total) + eps_small)).astype(BF))
    for step in range(STEPS):
        gram = [mm(x, x, TN).astype(BF) for x in ortho]
        square = [mm(g, g) for g in gram]
        poly = [(coef_b * g.astype(FP) + coef_c * s).astype(BF) for g, s in zip(gram, square)]
        mixed = [mm(x, p) for x, p in zip(ortho, poly)]
        ortho = [(coef_a * x.astype(FP) + m).astype(BF) for x, m in zip(ortho, mixed)]
    for kind in range(3):
        old = fast[kind].astype(FP)
        moved = old + eta_rate * ortho[kind].astype(FP)
        old_norm = jnp.sqrt(jnp.sum(old * old, -1, keepdims=True))
        new_norm = jnp.sqrt(jnp.sum(moved * moved, -1, keepdims=True)) + eps_small
        fresh[kind] = (moved * (old_norm / new_norm)).astype(BF)
    gain = own_gain(gains, where[0])

    @pl.when(where[8] == 0)
    def _():
        out[...] = decode(qry[...], fresh, gain)


def query_kernel(where, queries, w_query, own, message, other, heads):
    rows = mm(queries[...], w_query[...])
    for head in range(HEADS):
        heads[head] = unit(rows[:, head * HD : (head + 1) * HD]).astype(BF)
    n_qry = own.shape[0]
    own[...] = heads[where[0]]
    message[:n_qry] = heads[where[2]]
    message[n_qry:] = heads[where[3]]
    other[...] = heads[where[4]]


def output_kernel(where, begun, near, back, relayed, w_out, out):
    def part(rows, head):
        return mm(rows, w_out[pl.ds(pl.multiple_of(head * HD, HD), HD)])

    cross = jnp.where(where[8] == 0, back[: relayed.shape[0]], relayed[...])
    out[...] = (begun[...] + part(near[...], where[2]) + part(cross, where[5])).astype(BF)


def whole(shape):
    return pl.BlockSpec(shape, lambda i, where: (0,) * len(shape))


def call(kernel, where, args, outs, scratch=()):
    return pl.pallas_call(
        kernel,
        out_shape=outs,
        grid_spec=pltpu.PrefetchScalarGridSpec(
            num_scalar_prefetch=1,
            grid=(1,),
            in_specs=[whole(a.shape) for a in args],
            out_specs=jax.tree.map(lambda o: whole(o.shape), outs),
            scratch_shapes=scratch,
        ),
        compiler_params=pltpu.CompilerParams(vmem_limit_bytes=32 << 20),
    )(where, *args)


def local(tokens, w_kv, w_rate, fast_weights, queries, w_query, out_gain, w_out):
    n_patch, n_view, n_head = (lax.axis_size(a) for a in ("patch", "view", "head"))
    patch, view, core = (lax.axis_index(a) for a in ("patch", "view", "head"))
    n_tok, width = tokens.shape
    n_qry = queries.shape[0]
    side = view % 2
    first = core == 0
    head = jnp.where(first, 2 * side, 1)
    sibling = jnp.where(first, 1, 2 * side)
    second = jnp.where(first, 1, 2 - 2 * side)
    units = jnp.where(first, 0, side * LARGE), jnp.where(first, LARGE, LARGE + SMALL)
    where = [head, patch, sibling, second, 2 - 2 * side, 2 - 2 * side, head, 2 * side, core, side]
    where = jnp.stack(where).astype(jnp.int32)
    swap = [(0, 1), (1, 0)]

    def device(p, v, c):
        return (p * n_view + v) * n_head + c

    every = ("patch", "view", "head")
    ours = [(device(p, v, 0), device(p, v ^ 1, 0)) for p in range(n_patch) for v in range(n_view)]

    def rotate(n, shift):
        return [(i, (i + shift) % n) for i in range(n)]

    seconds = [(a + 1, b + 1) for a, b in ours]

    def pairs(s):
        return [(i, i ^ s) for i in range(n_patch)]

    far = [lax.ppermute(tokens, "view", rotate(n_view, s)) for s in range(1, n_view)]
    near = [tokens, lax.ppermute(tokens, "head", swap)]
    mine = lax.dynamic_index_in_dim(fast_weights, head, 2, keepdims=False).transpose(1, 0, 2)

    weights = [w_rate]
    for owner, unit_at, size in ((head, units[0], LARGE), (2 * side, units[1], SMALL)):
        weights.append(lax.dynamic_slice_in_dim(w_kv, owner * HD, HD, 1))
        weights.append(lax.dynamic_slice_in_dim(w_kv, width + owner * HD, HD, 1))
        piece = lax.dynamic_slice(fast_weights, (unit_at, 0, owner, 0), (size, 3, 1, HD))
        weights.append(piece.reshape(size, 3, HD).transpose(1, 0, 2))
    sums = [jax.ShapeDtypeStruct((3, size, HD), FP) for size in (LARGE, SMALL)]

    def held(toks):
        return [pltpu.VMEM((len(toks) * n_tok, HD), BF)] * 2

    begun = list(call(functools.partial(first_kernel, len(near)), where, near + weights, sums, held(near)))
    late, _ = lax.optimization_barrier((queries, begun[0]))
    own_qry, message, other = call(
        query_kernel,
        where,
        [late, w_query],
        [jax.ShapeDtypeStruct((n, HD), BF) for n in (n_qry, 2 * n_qry, n_qry)],
        [pltpu.VMEM((HEADS, n_qry, HD), BF)],
    )
    begun[0], message, *far = lax.optimization_barrier((begun[0], message, *far))
    far = far + [lax.ppermute(f, "head", swap) for f in far]
    message, far[-1] = lax.optimization_barrier((message, far[-1]))
    swapped = lax.ppermute(message, "head", swap)
    size = (LARGE + SMALL) // n_patch
    chunks = call(
        functools.partial(second_kernel, len(far), n_patch),
        where,
        far + weights + begun,
        [jax.ShapeDtypeStruct((3, size, HD), BF if k else FP) for k in range(n_patch)],
        [pltpu.VMEM(s.shape, FP) for s in sums] + held(far),
    )
    order = exchange_order(n_patch)
    got = [lax.ppermute(chunks[k], "patch", pairs(order[k])) for k in range(n_patch - 1, 0, -1)]
    own = chunks[0]
    for part in got:
        own = own + part.astype(FP)
    other, swapped, _ = lax.optimization_barrier((other, swapped, chunks[0]))
    across = lax.ppermute(jnp.concatenate([other, swapped[n_qry:]]), every, ours)
    own = own.astype(BF)
    parts = [lax.ppermute(own, "patch", pairs(s)) for s in exchange_order(n_patch, True)[1:]]
    parts[0], across = lax.optimization_barrier((parts[0], across))
    large, small = call(
        functools.partial(collect_kernel, n_patch),
        where,
        [own, *parts],
        [jax.ShapeDtypeStruct(s.shape, BF) for s in sums],
    )
    rest = lax.ppermute(small, "head", swap)
    large, rest = lax.optimization_barrier((large, rest))
    half = lax.ppermute(large, every, seconds)
    gains = out_gain.reshape(1, width)
    normed, fresh = call(
        far_kernel,
        where,
        [large, small, rest, half, mine, gains, across],
        [jax.ShapeDtypeStruct((2 * n_qry, HD), BF), jax.ShapeDtypeStruct((3, FF, HD), BF)],
        [pltpu.VMEM((3, FF, HD), BF)],
    )
    back = lax.ppermute(normed, every, ours)
    for_other, begun = call(
        near_kernel,
        where,
        [own_qry, swapped[:n_qry], fresh, gains, w_out],
        [jax.ShapeDtypeStruct((n_qry, HD), BF), jax.ShapeDtypeStruct((n_qry, width), FP)],
    )
    near_out = lax.ppermute(for_other, "head", swap)
    begun, back = lax.optimization_barrier((begun, back))
    relayed = lax.ppermute(back[n_qry:], "head", swap)
    return call(
        output_kernel,
        where,
        [begun, near_out, back, relayed, w_out],
        jax.ShapeDtypeStruct((n_qry, width), BF),
    )


def solution(mesh):
    split = P(("groups", "patch", "view", "head"), None)
    in_specs = (split, P(), P(), P(), split, P(), P(), P())
    return jax.shard_map(local, mesh=mesh, in_specs=in_specs, out_specs=split, check_vma=False)
```

```python
import functools
import jax
import jax.numpy as jnp
from jax import lax
from jax.experimental import pallas as pl
from jax.experimental.pallas import tpu as pltpu
from jax.sharding import PartitionSpec as P

HEADS = 3
HD = 256
FF = 512
STEPS = 3

coef_a = 3.4445
coef_b = -4.775
coef_c = 2.0315
eta_rate = 3.0
eps_small = 1e-06

FP = jnp.float32
BF = jnp.bfloat16
NT = (((1,), (1,)), ((), ()))
TN = (((0,), (0,)), ((), ()))
LARGE = FF // 2
SMALL = FF // 4


def exchange_order(n_patch, back=False):
    if n_patch < 4:
        return [*range(n_patch)]
    return [0, *((2, 1, 3) if back else (3, 1, 2)), *range(4, n_patch)]


def mm(a, b, dims=(((1,), (0,)), ((), ()))):
    return lax.dot_general(a, b, dims, preferred_element_type=FP)


def unit(raw):
    return raw * lax.rsqrt(jnp.sum(raw * raw, -1, keepdims=True) + eps_small)


def project(rows, head, w_k, w_v, w_rate, keys, scaled):
    keys[...] = unit(mm(rows, w_k[...])).astype(BF)
    rates = mm(rows, w_rate[...], NT)
    pick = lax.broadcasted_iota(jnp.int32, rates.shape, 1) == head
    rate = jnp.sum(jnp.where(pick, rates, 0.0), -1, keepdims=True)
    rate = jnp.maximum(rate, 0.0) + jnp.log1p(jnp.exp(-jnp.abs(rate)))
    scaled[...] = (rate * mm(rows, w_v[...])).astype(BF)


def gradient(keys, scaled, fast, begun, acc):
    gate_pre = mm(fast[0], keys, NT)
    up_pre = mm(fast[1], keys, NT)
    back = mm(fast[2], scaled, NT)
    sig = jax.nn.sigmoid(gate_pre)
    act = gate_pre * sig
    hidden = (act * up_pre).astype(BF)
    d_gate = (back * up_pre * sig * (1.0 + gate_pre * (1.0 - sig))).astype(BF)
    d_up = (back * act).astype(BF)
    for kind, (left, right) in enumerate(((d_gate, keys), (d_up, keys), (hidden, scaled))):
        product = mm(left, right)
        acc[kind] = product if begun is None else begun[kind] + product


def segments(where, toks, weights, begun, accs, keys, scaled):
    w_rate, *weights = weights
    large, small = weights[:3], weights[3:]
    rows = jnp.concatenate([tok[...] for tok in toks])
    project(rows, where[6], *large[:2], w_rate, keys, scaled)
    gradient(keys[...], scaled[...], large[2], begun[0], accs[0])

    @pl.when(where[8] != 0)
    def _():
        project(rows, where[7], *small[:2], w_rate, keys, scaled)

    gradient(keys[...], scaled[...], small[2], begun[1], accs[1])


def first_kernel(n_tok, where, *refs):
    toks, weights, accs, rows = refs[:n_tok], refs[n_tok:-4], refs[-4:-2], refs[-2:]
    segments(where, toks, weights, (None, None), accs, *rows)


def second_kernel(n_tok, n_patch, where, *refs):
    toks, weights, begun = refs[:n_tok], refs[n_tok : n_tok + 7], refs[n_tok + 7 : n_tok + 9]
    outs, accs, rows = refs[n_tok + 9 : -4], refs[-4:-2], refs[-2:]
    segments(where, toks, weights, begun, accs, *rows)
    for out, shift in zip(outs, exchange_order(n_patch)):
        chunk = where[1] ^ shift
        at = 0
        for acc in accs:
            size = acc.shape[1] // n_patch
            out[:, at : at + size] = acc[:, pl.ds(pl.multiple_of(chunk * size, size), size)].astype(out.dtype)
            at += size


def collect_kernel(n_patch, where, *refs):
    parts, (later, small) = refs[:n_patch], refs[n_patch:]
    large, rest = LARGE // n_patch, SMALL // n_patch
    for k, (part, shift) in enumerate(zip(parts, exchange_order(n_patch, True))):
        if k:
            later[:, (k - 1) * large : k * large] = part[:, :large]
        chunk = where[1] ^ shift
        small[:, pl.ds(pl.multiple_of(chunk * rest, rest), rest)] = part[:, large:]


def decode(rows, fresh, gain):
    gate_pre = mm(rows, fresh[0], NT)
    up_pre = mm(rows, fresh[1], NT)
    hidden = (gate_pre * jax.nn.sigmoid(gate_pre) * up_pre).astype(BF)
    read = mm(hidden, fresh[2])
    return (read * lax.rsqrt(jnp.mean(read * read, -1, keepdims=True) + eps_small) * gain).astype(BF)


def own_gain(gains, head):
    low, middle, high = (gains[:, i * HD : (i + 1) * HD] for i in range(HEADS))
    return jnp.where(head == 0, low, jnp.where(head == 1, middle, high)).astype(FP)


def near_kernel(where, own, other, fresh, gains, w_out, for_other, begun):
    gain = own_gain(gains, where[0])
    for_other[...] = decode(other[...], fresh, gain)
    product = w_out[pl.ds(pl.multiple_of(where[0] * HD, HD), HD)]
    begun[...] = mm(decode(own[...], fresh, gain), product)


def far_kernel(n_patch, where, own, later, own_other, later_other, small, rest, fast, gains, qry, out, fresh, grads):
    size = LARGE // n_patch

    def place(start, own, later):
        for k, shift in enumerate(exchange_order(n_patch, True)):
            rows = pl.ds(pl.multiple_of(start + (where[1] ^ shift) * size, size), size)
            grads[:, rows] = later[:, (k - 1) * size : k * size] if k else own[...]

    place(where[8] * where[9] * LARGE, own, later)

    @pl.when(where[8] == 0)
    def _():
        grads[:, LARGE : LARGE + SMALL] = small[...]
        grads[:, LARGE + SMALL :] = rest[...]

    @pl.when(where[8] == 1)
    def _():
        place((1 - where[9]) * LARGE, own_other, later_other)

    ortho = []
    for kind in range(3):
        grad = grads[kind].astype(FP)
        total = jnp.sum(jnp.sum(grad * grad, -1, keepdims=True), 0, keepdims=True)
        ortho.append((grad / (jnp.sqrt(total) + eps_small)).astype(BF))
    for step in range(STEPS):
        gram = [mm(x, x, TN).astype(BF) for x in ortho]
        square = [mm(g, g) for g in gram]
        poly = [(coef_b * g.astype(FP) + coef_c * s).astype(BF) for g, s in zip(gram, square)]
        mixed = [mm(x, p) for x, p in zip(ortho, poly)]
        ortho = [(coef_a * x.astype(FP) + m).astype(BF) for x, m in zip(ortho, mixed)]
    for kind in range(3):
        old = fast[kind].astype(FP)
        moved = old + eta_rate * ortho[kind].astype(FP)
        old_norm = jnp.sqrt(jnp.sum(old * old, -1, keepdims=True))
        new_norm = jnp.sqrt(jnp.sum(moved * moved, -1, keepdims=True)) + eps_small
        fresh[kind] = (moved * (old_norm / new_norm)).astype(BF)
    gain = own_gain(gains, where[0])

    @pl.when(where[8] == 0)
    def _():
        out[...] = decode(qry[...], fresh, gain)


def query_kernel(where, queries, w_query, own, message, other, heads):
    rows = mm(queries[...], w_query[...])
    for head in range(HEADS):
        heads[head] = unit(rows[:, head * HD : (head + 1) * HD]).astype(BF)
    n_qry = own.shape[0]
    own[...] = heads[where[0]]
    message[:n_qry] = heads[where[2]]
    message[n_qry:] = heads[where[3]]
    other[...] = heads[where[4]]


def output_kernel(where, begun, near, back, relayed, w_out, out):
    def part(rows, head):
        return mm(rows, w_out[pl.ds(pl.multiple_of(head * HD, HD), HD)])

    cross = jnp.where(where[8] == 0, back[: relayed.shape[0]], relayed[...])
    out[...] = (begun[...] + part(near[...], where[2]) + part(cross, where[5])).astype(BF)


def whole(shape):
    return pl.BlockSpec(shape, lambda i, where: (0,) * len(shape))


def call(kernel, where, args, outs, scratch=()):
    return pl.pallas_call(
        kernel,
        out_shape=outs,
        grid_spec=pltpu.PrefetchScalarGridSpec(
            num_scalar_prefetch=1,
            grid=(1,),
            in_specs=[whole(a.shape) for a in args],
            out_specs=jax.tree.map(lambda o: whole(o.shape), outs),
            scratch_shapes=scratch,
        ),
        compiler_params=pltpu.CompilerParams(vmem_limit_bytes=32 << 20),
    )(where, *args)


def local(tokens, w_kv, w_rate, fast_weights, queries, w_query, out_gain, w_out):
    n_patch, n_view, n_head = (lax.axis_size(a) for a in ("patch", "view", "head"))
    patch, view, core = (lax.axis_index(a) for a in ("patch", "view", "head"))
    n_tok, width = tokens.shape
    n_qry = queries.shape[0]
    side = view % 2
    first = core == 0
    head = jnp.where(first, 2 * side, 1)
    sibling = jnp.where(first, 1, 2 * side)
    second = jnp.where(first, 1, 2 - 2 * side)
    units = jnp.where(first, 0, side * LARGE), jnp.where(first, LARGE, LARGE + SMALL)
    where = [head, patch, sibling, second, 2 - 2 * side, 2 - 2 * side, head, 2 * side, core, side]
    where = jnp.stack(where).astype(jnp.int32)
    swap = [(0, 1), (1, 0)]

    def device(p, v, c):
        return (p * n_view + v) * n_head + c

    every = ("patch", "view", "head")
    ours = [(device(p, v, 0), device(p, v ^ 1, 0)) for p in range(n_patch) for v in range(n_view)]

    def rotate(n, shift):
        return [(i, (i + shift) % n) for i in range(n)]

    seconds = [(a + 1, b + 1) for a, b in ours]

    def pairs(s):
        return [(i, i ^ s) for i in range(n_patch)]

    far = [lax.ppermute(tokens, "view", rotate(n_view, s)) for s in range(1, n_view)]
    near = [tokens, lax.ppermute(tokens, "head", swap)]
    mine = lax.dynamic_index_in_dim(fast_weights, head, 2, keepdims=False).transpose(1, 0, 2)

    weights = [w_rate]
    for owner, unit_at, size in ((head, units[0], LARGE), (2 * side, units[1], SMALL)):
        weights.append(lax.dynamic_slice_in_dim(w_kv, owner * HD, HD, 1))
        weights.append(lax.dynamic_slice_in_dim(w_kv, width + owner * HD, HD, 1))
        piece = lax.dynamic_slice(fast_weights, (unit_at, 0, owner, 0), (size, 3, 1, HD))
        weights.append(piece.reshape(size, 3, HD).transpose(1, 0, 2))
    sums = [jax.ShapeDtypeStruct((3, size, HD), FP) for size in (LARGE, SMALL)]

    def held(toks):
        return [pltpu.VMEM((len(toks) * n_tok, HD), BF)] * 2

    begun = list(call(functools.partial(first_kernel, len(near)), where, near + weights, sums, held(near)))
    late, _ = lax.optimization_barrier((queries, begun[0]))
    own_qry, message, other = call(
        query_kernel,
        where,
        [late, w_query],
        [jax.ShapeDtypeStruct((n, HD), BF) for n in (n_qry, 2 * n_qry, n_qry)],
        [pltpu.VMEM((HEADS, n_qry, HD), BF)],
    )
    begun[0], message, *far = lax.optimization_barrier((begun[0], message, *far))
    far = far + [lax.ppermute(f, "head", swap) for f in far]
    message, far[-1] = lax.optimization_barrier((message, far[-1]))
    swapped = lax.ppermute(message, "head", swap)
    size = (LARGE + SMALL) // n_patch
    chunks = call(
        functools.partial(second_kernel, len(far), n_patch),
        where,
        far + weights + begun,
        [jax.ShapeDtypeStruct((3, size, HD), BF if k else FP) for k in range(n_patch)],
        [pltpu.VMEM(s.shape, FP) for s in sums] + held(far),
    )
    order = exchange_order(n_patch)
    got = [lax.ppermute(chunks[k], "patch", pairs(order[k])) for k in range(n_patch - 1, 0, -1)]
    own = chunks[0]
    for part in got:
        own = own + part.astype(FP)
    other, swapped, _ = lax.optimization_barrier((other, swapped, chunks[0]))
    across = lax.ppermute(jnp.concatenate([other, swapped[n_qry:]]), every, ours)
    own = own.astype(BF)
    parts = [lax.ppermute(own, "patch", pairs(s)) for s in exchange_order(n_patch, True)[1:]]
    own_large = own[:, : LARGE // n_patch]
    own_other = lax.ppermute(own_large, every, seconds)
    parts[0], across, own_other = lax.optimization_barrier((parts[0], across, own_other))
    later, small = call(
        functools.partial(collect_kernel, n_patch),
        where,
        [own, *parts],
        [jax.ShapeDtypeStruct((3, n, HD), BF) for n in (LARGE - LARGE // n_patch, SMALL)],
    )
    rest = lax.ppermute(small, "head", swap)
    later, rest = lax.optimization_barrier((later, rest))
    later_other = lax.ppermute(later, every, seconds)
    gains = out_gain.reshape(1, width)
    normed, fresh = call(
        functools.partial(far_kernel, n_patch),
        where,
        [own_large, later, own_other, later_other, small, rest, mine, gains, across],
        [jax.ShapeDtypeStruct((2 * n_qry, HD), BF), jax.ShapeDtypeStruct((3, FF, HD), BF)],
        [pltpu.VMEM((3, FF, HD), BF)],
    )
    back = lax.ppermute(normed, every, ours)
    for_other, begun = call(
        near_kernel,
        where,
        [own_qry, swapped[:n_qry], fresh, gains, w_out],
        [jax.ShapeDtypeStruct((n_qry, HD), BF), jax.ShapeDtypeStruct((n_qry, width), FP)],
    )
    near_out = lax.ppermute(for_other, "head", swap)
    begun, back = lax.optimization_barrier((begun, back))
    relayed = lax.ppermute(back[n_qry:], "head", swap)
    return call(
        output_kernel,
        where,
        [begun, near_out, back, relayed, w_out],
        jax.ShapeDtypeStruct((n_qry, width), BF),
    )


def solution(mesh):
    split = P(("groups", "patch", "view", "head"), None)
    in_specs = (split, P(), P(), P(), split, P(), P(), P())
    return jax.shard_map(local, mesh=mesh, in_specs=in_specs, out_specs=split, check_vma=False)
```
